32 devices in a mesh: leaf: 2 (over x), row: 4 (over y, core), col: 4 (over z).
Axes of the slice: x: 2, y: 2, z: 4, core: 2. Of those that a mesh axis runs over, the one named last changes fastest.
Arguments:
- leaf_front: float32 [2, 7, 4, 128, 7, 4, 128], P('leaf', None, 'row', None, None, 'col'), as said below
- leaf_pattern: int32 [2, 28, 28], P('leaf'), may hold values from 0 to 1, as said below
- parent_panel: float32 [1, 2, 7, 4, 128, 4, 128], P(None, 'leaf', None, 'row', None, 'col'), may hold values from -0.125 to 0.125
- parent_diag: float32 [1, 2, 7, 4, 128], P(None, 'leaf', None, 'row'), may hold values from 1.5 to 2.5
- parent_pattern: int32 [1, 2, 28, 28], replicated, may hold values from 0 to 1, as said below
- ext_map: int32 [1, 2, 24], replicated, may hold values from 0 to 27, as said below
Outputs:
- panels: float32 [2, 2, 7, 4, 128, 4, 128], P(None, 'leaf', None, 'row', None, 'col')
- top_update: float32 [2, 6, 4, 128, 6, 4, 128], P('leaf', None, 'row', None, None, 'col')
The draws below stay inside these ranges and needn't reach their ends.
Inputs may be any that keep to these rules, and one draw needn't show every extreme that they name: Each leaf_front[g], read as a matrix, is symmetric; every front built in the reference program is positive definite. leaf_pattern: symmetric, with every diagonal block 1. parent_pattern: symmetric, with every diagonal block 1. parent_pattern[d, n] belongs to node n at depth d+1; rows n of 2 / 2^(d+1) or more are not read. ext_map[d, n] belongs to node n at depth d; rows n of 2 / 2^d or more are not read. Along its 24 entries it rises strictly; ext_map[d, n, j] - j is the same for the 4 entries j of each aligned run of 4, never falls and lies in 0 to 4. Among the entries j of one class of j mod 4, at most two lie in one class of ext_map mod 4, and in every row some two do.
All inputs are finite; a program needn't handle non-finite values.
Results may differ from the reference program's by a relative error of at most 0.0003.
Values sent between devices are 32-bit elements; how exact they have to be, the bound alone decides.
A program may use at most 128 MiB of HBM per device.

```python
import math
import jax
import jax.numpy as jnp
import numpy as np
from jax import lax

BLOCK = 128
FRONT = 3584
PIVOTS = 512
FRONT_BLOCKS = 28
CONTRIB = 3072
CONTRIB_BLOCKS = 24
BLOCK_ROWS = 7
CONTRIB_ROWS = 6
LEVELS = 1
N_LEAF = 2
N_ROW = 4
N_COL = 4


size_table = np.array([[count_a, count_b, count_c, count_d, count_e] for count_a in range(3) for count_b in range(3) for count_c in range(3) for count_d in range(3) for count_e in range(3) if count_a + count_b + count_c + count_d + count_e == 6 and count_a + count_e <= 2], dtype=np.int32)


def draw_leaf_front(key, part):

    def draw_single(sub_key):
        random_part = jax.random.normal(sub_key, (FRONT, FRONT), jnp.float32)
        diagonal = jax.random.uniform(jax.random.fold_in(sub_key, 1), (FRONT,), jnp.float32, 0.9, 1.5)
        spread_scale = 0.35 / math.sqrt(2.0 * FRONT)
        return (random_part + random_part.T) * spread_scale + jnp.diag(diagonal)
    leaf_keys = jax.random.split(jax.random.fold_in(key, 7), N_LEAF)
    fronts = lax.map(draw_single, leaf_keys)
    return fronts.reshape(N_LEAF, BLOCK_ROWS, N_ROW, BLOCK, BLOCK_ROWS, N_COL, BLOCK)


def pattern_draw(key, leading):
    tosses = jax.random.randint(key, leading + (FRONT_BLOCKS, FRONT_BLOCKS), 0, 5, dtype=jnp.int32)
    row_ids = jnp.arange(FRONT_BLOCKS)[:, None]
    col_ids = jnp.arange(FRONT_BLOCKS)[None, :]
    lower_part = jnp.where(row_ids > col_ids, (tosses < 3).astype(jnp.int32), 0)
    return lower_part + jnp.swapaxes(lower_part, -1, -2) + (row_ids == col_ids).astype(jnp.int32)


def draw_leaf_pattern(key, part):
    return pattern_draw(jax.random.fold_in(key, 11), (N_LEAF,))


def draw_parent_pattern(key, part):
    return pattern_draw(jax.random.fold_in(key, 13), (LEVELS, N_LEAF))


def draw_ext_map(key, part):
    table = jnp.asarray(size_table)
    chosen = jax.random.randint(jax.random.fold_in(key, 17), (LEVELS, N_LEAF), 0, table.shape[0], dtype=jnp.int32)
    counts = table[chosen]
    bounds = jnp.cumsum(counts, axis=-1)
    quad_index = jnp.arange(CONTRIB_BLOCKS // N_ROW, dtype=jnp.int32)
    offsets = jnp.sum((bounds[..., None, :] <= quad_index[:, None]).astype(jnp.int32), axis=-1)
    return jnp.arange(CONTRIB_BLOCKS, dtype=jnp.int32) + jnp.repeat(offsets, N_ROW, axis=-1)


def shard_levels(rng, shape, cuts, low, high):
    factor_of = 1.0
    for axis_at, parts in cuts:
        heights = jax.random.uniform(jax.random.fold_in(jax.random.fold_in(rng, 6), axis_at), (parts,), jnp.float32, low / len(cuts), high / len(cuts))
        factor_of = factor_of * jnp.repeat(jnp.exp(heights), shape[axis_at] // parts).reshape((-1,) + (1,) * (len(shape) - 1 - axis_at))
    return factor_of


def noise(rng, dims, scale, limit, cuts=(), held_as=jnp.bfloat16):
    drawn = scale * jax.random.normal(rng, dims, jnp.float32)
    if cuts:
        drawn = drawn * shard_levels(rng, dims, cuts, -0.22, 0.18)
    return jnp.clip(drawn, -limit, limit).astype(held_as)


def setup_inputs(seed: int = 0) -> dict:
    key_list = jax.random.split(jax.random.key(seed), 7)
    return {
        "leaf_front": draw_leaf_front(jax.random.fold_in(key_list[6], 71), 0),
        "leaf_pattern": draw_leaf_pattern(jax.random.fold_in(key_list[6], 71), 0),
        "parent_panel": noise(key_list[2], (LEVELS, N_LEAF, BLOCK_ROWS, N_ROW, BLOCK, N_COL, BLOCK), (FRONT * 2 // 3) ** -0.5, 0.125, ((1, 2), (3, 4), (5, 4)), jnp.float32),
        "parent_diag": jnp.clip(1.5 + 1.0 * jax.random.uniform(key_list[3], (LEVELS, N_LEAF, BLOCK_ROWS, N_ROW, BLOCK), jnp.float32) ** shard_levels(key_list[3], (LEVELS, N_LEAF, BLOCK_ROWS, N_ROW, BLOCK), ((1, 2), (3, 4)), -0.2, 0.2), 1.5, 2.5),
        "parent_pattern": draw_parent_pattern(jax.random.fold_in(key_list[6], 71), 0),
        "ext_map": draw_ext_map(jax.random.fold_in(key_list[6], 71), 0),
    }


highest = lax.Precision.HIGHEST

def symmetric_lower(matrix):
    return jnp.tril(matrix) + jnp.swapaxes(jnp.tril(matrix, -1), -1, -2)

def partial_factor(front):
    symmetric = symmetric_lower(front)
    pivot_factor = jnp.linalg.cholesky(symmetric[:PIVOTS, :PIVOTS])
    lower_rows = lax.linalg.triangular_solve(pivot_factor, symmetric[PIVOTS:, :PIVOTS], left_side=False, lower=True, transpose_a=True)
    update = symmetric[PIVOTS:, PIVOTS:] - jnp.dot(lower_rows.astype(jnp.float32), lower_rows.T.astype(jnp.float32), precision=highest, preferred_element_type=jnp.float32)
    panel_col = jnp.concatenate([pivot_factor, lower_rows], axis=0)
    return (panel_col, update)

def block_mask(pattern):
    return jnp.repeat(jnp.repeat(pattern.astype(jnp.float32), BLOCK, axis=0), BLOCK, axis=1)

def extend_add(front, update, child_map):
    positions = (child_map[:, None] * BLOCK + jnp.arange(BLOCK, dtype=jnp.int32)[None, :]).reshape(-1).astype(jnp.int32)
    return front.at[positions[:, None], positions[None, :]].add(update)

def reference(leaf_front, leaf_pattern, parent_panel, parent_diag, parent_pattern, ext_map):
    leaves = leaf_front.reshape(N_LEAF, FRONT, FRONT)

    def leaf_step(members):
        front, pattern = members
        return partial_factor(block_mask(pattern) * front)
    panels_now, updates = lax.map(leaf_step, (leaves, leaf_pattern))
    panel_list = [panels_now]
    for depth in range(LEVELS):
        node_count = N_LEAF >> depth + 1
        group_span = 2 ** (depth + 1)
        shares = parent_panel[depth].reshape(node_count, group_span, FRONT, PIVOTS).sum(axis=1)
        diagonals = parent_diag[depth].reshape(node_count, group_span, FRONT).sum(axis=1)
        child_maps = ext_map[depth, :2 * node_count].reshape(node_count, 2, CONTRIB_BLOCKS)
        child_updates = updates.reshape(node_count, 2, CONTRIB, CONTRIB)
        patterns = parent_pattern[depth, :node_count]

        def node_step(members):
            share, diagonal, pattern, maps_here, children = members
            initials = jnp.concatenate([share, jnp.zeros((FRONT, FRONT - PIVOTS), jnp.float32)], axis=1) + jnp.diag(diagonal)
            front = block_mask(pattern) * initials
            front = extend_add(front, children[0], maps_here[0])
            front = extend_add(front, children[1], maps_here[1])
            return partial_factor(front)
        panels_now, updates = lax.map(node_step, (shares, diagonals, patterns, child_maps, child_updates))
        panel_list.append(panels_now)
    stacked = jnp.stack([jnp.repeat(panel_set, 2 ** depth, axis=0) for depth, panel_set in enumerate(panel_list)])
    panels = stacked.reshape(LEVELS + 1, N_LEAF, BLOCK_ROWS, N_ROW, BLOCK, N_COL, BLOCK)
    top_update = jnp.repeat(jnp.tril(updates), 2 ** LEVELS, axis=0).reshape(N_LEAF, CONTRIB_ROWS, N_ROW, BLOCK, CONTRIB_ROWS, N_COL, BLOCK)
    return (panels, top_update)
```

```python
import functools
import jax
import jax.numpy as jnp
from jax import lax
from jax.experimental import pallas as pl
from jax.experimental.pallas import tpu as pltpu
from jax.sharding import PartitionSpec as P

highest = lax.Precision.HIGHEST
MESH = pl.DeviceIdType.MESH
f32 = jnp.float32
bf16 = jnp.bfloat16


def symmetric_lower(matrix):
    size = matrix.shape[0]
    row = lax.broadcasted_iota(jnp.int32, (size, size), 0)
    col = lax.broadcasted_iota(jnp.int32, (size, size), 1)
    return jnp.where(row >= col, matrix, matrix.T)


def eliminate_block(block):
    size = block.shape[0]
    groups = size // 8
    lane = lax.broadcasted_iota(jnp.int32, (8, size), 1)
    sub = lax.broadcasted_iota(jnp.int32, (8, size), 0)
    rows = [block[8 * g : 8 * g + 8, :] for g in range(groups)]
    for g in range(groups):
        base = 8 * g
        here = rows[g]
        inside = jnp.logical_and(lane >= base, lane < base + 8)
        line = [jnp.broadcast_to(here[a : a + 1, :], (8, size)) for a in range(8)]
        s = [
            [
                jnp.broadcast_to(line[a][:, base + b : base + b + 1], (8, size)) if b >= a else None
                for b in range(8)
            ]
            for a in range(8)
        ]
        line = [
            jnp.where(inside, jnp.where(lane == base + a, 1.0, 0.0), line[a]) for a in range(8)
        ]
        inverse = [None] * 8
        ratio = [[None] * 8 for _ in range(8)]
        for a in range(8):
            inverse[a] = 1.0 / s[a][a]
            for b in range(a + 1, 8):
                ratio[a][b] = s[a][b] * inverse[a]
            for b in range(a + 1, 8):
                for c in range(b, 8):
                    s[b][c] = s[b][c] - ratio[a][b] * s[a][c]
                line[b] = line[b] - ratio[a][b] * line[a]
        done = line[0]
        for a in range(8):
            whole = line[a]
            for b in range(a, 8):
                whole = jnp.where(lane == base + b, s[a][b], whole)
            done = whole if a == 0 else jnp.where(sub == a, whole, done)
        rows[g] = done
        if g + 1 < groups:
            solved = [None] * 8
            for a in range(7, -1, -1):
                total = line[a] * inverse[a]
                for b in range(a + 1, 8):
                    total = total - ratio[a][b] * solved[b]
                solved[a] = total
            for h in range(g + 1, groups):
                before = rows[h]
                total = jnp.where(inside, 0.0, before)
                for a in range(8):
                    spread = jnp.broadcast_to(before[:, base + a : base + a + 1], (8, size))
                    total = total - spread * solved[a]
                rows[h] = total
    return jnp.concatenate(rows, axis=0)


def pivot_step(start, block_size, inverse_ref, upper_ref, row_ref):
    order = inverse_ref.shape[0]
    row_id = lax.broadcasted_iota(jnp.int32, (block_size, block_size), 0)
    col_id = lax.broadcasted_iota(jnp.int32, (block_size, block_size), 1)
    wide_col = lax.broadcasted_iota(jnp.int32, (block_size, order), 1)
    tall_row = lax.broadcasted_iota(jnp.int32, (order, block_size), 0)
    here = pl.ds(start, block_size)
    reduced = eliminate_block(inverse_ref[here, here])
    pivot = jnp.sum(jnp.where(row_id == col_id, reduced, 0.0), axis=1, keepdims=True)
    scale = lax.rsqrt(pivot)
    scale = scale * (1.5 - 0.5 * pivot * scale * scale)
    scaled = reduced * scale
    small = jnp.where(row_id > col_id, scaled, jnp.where(row_id == col_id, scale, 0.0))
    row = jnp.dot(small, inverse_ref[here, :], precision=highest, preferred_element_type=f32)
    right = jnp.where(wide_col >= start + block_size, row, 0.0)
    upper_ref[here, :] = right
    upper_ref[here, here] = jnp.where(row_id <= col_id, scaled, 0.0)
    row_ref[...] = row
    row_ref[:, here] = small
    inverse_ref[:, here] = jnp.where(tall_row >= start + block_size, 0.0, inverse_ref[:, here])
    inverse_ref[...] = inverse_ref[...] - lax.dot_general(
        right,
        row_ref[...],
        (((0,), (0,)), ((), ())),
        precision=highest,
        preferred_element_type=f32,
    )
    inverse_ref[here, :] = jnp.where(wide_col < start + block_size, row_ref[...], 0.0)


def split(value):
    high = value.astype(bf16)
    return high, (value - high.astype(f32)).astype(bf16)


def product(left, right):
    dims = (((1,), (1,)), ((), ()))
    pairs = ((left[1], right[0]), (left[0], right[1]), (left[0], right[0]))
    parts = [lax.dot_general(a, b, dims, preferred_element_type=f32) for a, b in pairs]
    return (parts[0] + parts[1]) + parts[2]


def run(when, act):
    if when is True:
        act()
    else:
        pl.when(when)(act)


class Group:
    def __init__(self, side, rows, size, wide, sems):
        self.side, self.rows, self.size, self.wide = side, rows, size, wide
        self.p = lax.axis_index("row")
        self.q = lax.axis_index("col")
        self.core = self.p + 1 - 2 * lax.rem(self.p, 2)
        self.far = lax.rem(self.p + side // 2, side)
        self.diagonal = lax.rem(self.core + side // 2, side)
        self.sems = sems
        self.sent = []

    def columns(self, source):
        return pl.ds(pl.multiple_of(source * self.size, self.size), self.size)

    def copy(self, source, target, send, receive, place):
        return pltpu.make_async_remote_copy(
            src_ref=source,
            dst_ref=target,
            send_sem=send,
            recv_sem=receive,
            device_id=place,
            device_id_type=MESH,
        )

    def start(self, when, make):
        run(when, lambda: make().start())
        self.sent.append((when, make))

    def finish(self):
        for when, make in self.sent:
            run(when, lambda: make().wait_send())
        self.sent = []

    def spot(self, row, source, part):
        if part == "corner":
            return self.wide.at[row, 0, :, self.columns(source)]
        return self.wide.at[row, 1 : self.rows, :, self.columns(source)]

    def strip(self, row):
        return self.wide.at[row, 0]


def gather_corner(group, column):
    p, q, side = group.p, group.q, group.side
    z_send, z_recv, s_send, s_recv = group.sems[:4]
    group.wide[p, 0, :, group.columns(q)] = column[0]
    for hop in range(1, side):
        to = lax.rem(q + hop, side)

        def make(to=to, hop=hop):
            return group.copy(
                column.at[0],
                group.spot(p, q, "corner"),
                z_send.at[hop],
                z_recv.at[q],
                {"col": to},
            )

        group.start(True, make)


def gather_strips(group):
    p, q, side = group.p, group.q, group.side
    z_send, z_recv, s_send, s_recv = group.sems[:4]
    for hop in range(1, side):
        source = lax.rem(q + hop, side)
        spot = group.spot(p, source, "corner")
        group.copy(spot, spot, z_send.at[0], z_recv.at[source], {"col": q}).wait_recv()
    for index, place in ((0, group.core), (1, group.far)):

        def make(index=index, place=place):
            return group.copy(
                group.strip(p), group.strip(p), s_send.at[index], s_recv.at[index], {"row": place}
            )

        group.start(True, make)

    def wait(index, row):
        group.copy(
            group.strip(row), group.strip(row), s_send.at[index], s_recv.at[index], {"row": p}
        ).wait_recv()

    wait(1, group.far)

    def make():
        return group.copy(
            group.strip(group.far),
            group.strip(group.far),
            s_send.at[2],
            s_recv.at[2],
            {"row": group.core},
        )

    group.start(True, make)
    wait(0, group.core)
    wait(2, group.diagonal)


def load_corner(group, inverse_ref):
    side, size = group.side, group.size
    for row in range(side):
        for col in range(row + 1):
            block = group.wide[row, 0, :, col * size : (col + 1) * size]
            if row == col:
                inverse_ref[row * size : (row + 1) * size, col * size : (col + 1) * size] = (
                    symmetric_lower(block)
                )
            else:
                inverse_ref[row * size : (row + 1) * size, col * size : (col + 1) * size] = block
                inverse_ref[col * size : (col + 1) * size, row * size : (row + 1) * size] = block.T


class Lines:
    def __init__(self, group, column, every):
        self.group, self.column, self.every = group, column, every

    def wanted(self, row):
        return True if self.every else row == self.group.q

    def both(self, *conditions):
        kept = [c for c in conditions if c is not True]
        return functools.reduce(jnp.logical_and, kept) if kept else True

    def inside(self, source):
        return jnp.logical_and(source >= 0, source < self.group.side)

    def hop(self, step, act):
        g = self.group
        send, receive = g.sems[4:6]
        for index, sign in ((0, 1), (1, -1)):
            source = g.q - sign * (step - 1)
            to = g.q + sign

            def make(index=index, source=source, to=to):
                spot = g.spot(g.p, source, "lines")
                return g.copy(
                    spot, spot, send.at[2 * (step - 1) + index], receive.at[source], {"col": to}
                )

            when = jnp.logical_and(self.inside(source), self.inside(to))
            run(when, lambda: act(make()))

    def arrive(self, step):
        g = self.group
        send, receive = g.sems[4:6]
        for sign in (1, -1):
            source = g.q - sign * step

            def wait(source=source):
                spot = g.spot(g.p, source, "lines")
                g.copy(spot, spot, send.at[0], receive.at[source], {"col": g.q}).wait_recv()

            run(self.inside(source), wait)

    def sources(self, step):
        out = []
        for sign in (1, -1):
            source = self.group.q - sign * step
            valid = self.inside(source)
            if sign < 0:
                valid = jnp.logical_and(valid, step > 0)
            out.append((valid, source))
        return out

    def across(self, step, act):
        g = self.group
        send, receive = g.sems[6:8]
        for valid, source in self.sources(step):
            for index, place in ((0, g.far), (1, g.core)):

                def make(index=index, place=place, source=source):
                    spot = g.spot(g.p, source, "lines")
                    return g.copy(
                        spot,
                        spot,
                        send.at[index, source],
                        receive.at[index, source],
                        {"row": place},
                    )

                run(self.both(valid, self.wanted(g.p)), lambda: act(make()))

    def pass_on(self, step, act, first):
        g = self.group
        send, receive = g.sems[6:8]
        for valid, source in self.sources(step):

            def make(source=source):
                spot = g.spot(g.far, source, "lines")
                return g.copy(
                    spot, spot, send.at[2, source], receive.at[2, source], {"row": g.core}
                )

            def whole(source=source, make=make):
                if first:
                    spot = g.spot(g.far, source, "lines")
                    g.copy(
                        spot, spot, send.at[0, source], receive.at[0, source], {"row": g.p}
                    ).wait_recv()
                act(make())

            run(self.both(valid, self.wanted(g.far)), whole)

    def last(self):
        g = self.group
        send, receive = g.sems[6:8]
        for index, row in ((1, g.core), (2, g.diagonal)):
            for source in range(g.side):

                def wait(index=index, row=row, source=source):
                    spot = g.spot(row, source, "lines")
                    g.copy(
                        spot,
                        spot,
                        send.at[index, source],
                        receive.at[index, source],
                        {"row": g.p},
                    ).wait_recv()

                run(self.wanted(row), wait)

    def open(self):
        self.hop(1, begin)
        self.across(0, begin)

    def advance(self, step):
        side = self.group.side

        @pl.when(step + 1 < side)
        def _():
            self.arrive(step + 1)

            @pl.when(step + 2 < side)
            def _():
                self.hop(step + 2, begin)

            self.across(step + 1, begin)

        self.pass_on(step, begin, True)

    def finish(self):
        def body(step, carry):
            pl.when(step > 0)(lambda: self.hop(step, settle))
            self.across(step, settle)
            self.pass_on(step, settle, False)
            return carry

        lax.fori_loop(0, self.group.side, body, 0)


def begin(copy):
    copy.start()


def settle(copy):
    copy.wait_send()


def gather_sems(side):
    return [
        pltpu.SemaphoreType.DMA((side,)),
        pltpu.SemaphoreType.DMA((side,)),
        pltpu.SemaphoreType.DMA((3,)),
        pltpu.SemaphoreType.DMA((3,)),
        pltpu.SemaphoreType.DMA((2 * side,)),
        pltpu.SemaphoreType.DMA((side,)),
        pltpu.SemaphoreType.DMA((3, side)),
        pltpu.SemaphoreType.DMA((3, side)),
    ]


def meet(places):
    barrier = pltpu.get_barrier_semaphore()
    for place in places:
        pl.semaphore_signal(barrier, inc=1, device_id=place, device_id_type=MESH)
    pl.semaphore_wait(barrier, len(places))


def top_block(upper_ref, p, q, size):
    block = upper_ref[
        pl.ds(pl.multiple_of(q * size, size), size), pl.ds(pl.multiple_of(p * size, size), size)
    ]
    return jnp.where(p >= q, block.T, 0.0)


def tri(row, col, rows):
    return col * rows - col * (col - 1) // 2 + row - col


def factor(group, lines, inverse, upper, row_ref, extra):
    size = group.size

    def body(step, carry):
        pivot_step(pl.multiple_of(step * size, size), size, inverse, upper, row_ref)
        lines.advance(step)
        extra(step)
        return carry

    lax.fori_loop(0, group.side, body, 0)


def child_kernel(
    packed,
    node,
    map_ref,
    mask_ref,
    above_ref,
    front,
    share_ref,
    diag_ref,
    panel_ref,
    part_ref,
    column,
    inner,
    pack,
    recv,
    wide,
    inverse,
    upper,
    row_ref,
    inv_hi,
    inv_lo,
    tall,
    l_hi,
    l_lo,
    load_sem,
    f_send,
    f_recv,
    *sems,
):
    child, parent = node
    rows, size = column.shape[0], column.shape[1]
    runs = rows - 1
    side = wide.shape[0]
    group = Group(side, rows, size, wide, sems)
    p, q = group.p, group.q

    def block_of(t, u):
        if packed:
            return front.at[tri(t, u, rows)]
        return front.at[0, t, 0, :, u, 0, :]

    def place_of(t, u):
        return column.at[t] if u == 0 else inner.at[(t - 1) * runs + u - 1]

    spots = [(t, u) for u in range(rows) for t in range(u, rows)]
    loads = [
        pltpu.make_async_copy(block_of(t, u), place_of(t, u), load_sem.at[index])
        for index, (t, u) in enumerate(spots)
    ]
    for load in loads:
        load.start()
    others = []
    for r in range(side):
        for c in range(side):
            if r or c:
                others.append({"row": lax.rem(p + r, side), "col": lax.rem(q + c, side)})
    meet(others)

    def masked(t, u):
        if packed:
            return 1.0
        return mask_ref[side * t + p, side * u + q].astype(f32)

    loads[0].wait()
    column[0] = column[0] * masked(0, 0)
    gather_corner(group, column)
    for t in range(1, rows):
        loads[t].wait()
        column[t] = column[t] * masked(t, 0)
    wide[p, 1:rows, :, group.columns(q)] = column[1:rows]
    lines = Lines(group, column, True)
    lines.open()
    for index in range(rows, len(spots)):
        loads[index].wait()

    shift = [jnp.clip(map_ref[child, side * k] - side * k, 0, side) for k in range(runs)]
    kind = [lax.rem(s, side) for s in shift]
    rank = []
    for k in range(runs):
        count = jnp.int32(0)
        for j in range(k):
            count = count + jnp.where(kind[j] == kind[k], 1, 0)
        rank.append(jnp.minimum(count, 1))
    chosen = []
    for r in range(side):
        pair = []
        for i in range(2):
            found = jnp.int32(0)
            for k in range(runs):
                hit = jnp.logical_and(kind[k] == r, rank[k] == i)
                found = jnp.where(hit, k, found)
            pair.append(found)
        chosen.append(pair)

    def slots_of(r, c):
        if r == c:
            return [(0, 0), (1, 0), (1, 1)]
        if 1 <= r < c:
            return []
        return [(0, 0), (0, 1), (1, 0), (1, 1)]

    moves = []
    for c in range(side):
        for r in range(side):
            slots = slots_of(r, c)
            if not slots:
                continue
            for slot, (i, j) in enumerate(slots):
                k, l = chosen[r][i], chosen[c][j]
                k, l = jnp.maximum(k, l), jnp.minimum(k, l)
                block = inner[k * runs + l]
                if not packed:
                    block = block * mask_ref[side * (k + 1) + p, side * (l + 1) + q].astype(f32)
                if r or c:
                    pack[r * side + c, slot] = block
                else:
                    recv[0, slot] = block
            if r or c:
                moves.append((r, c, len(slots)))

    def move(r, c, count):
        index = r * side + c
        return lambda: group.copy(
            pack.at[index, 0:count],
            recv.at[index, 0:count],
            f_send.at[index],
            f_recv.at[index],
            {"row": lax.rem(p + r, side), "col": lax.rem(q + c, side)},
        )

    gather_strips(group)
    load_corner(group, inverse)
    order = sorted(moves, key=lambda m: -min(m[1], side - m[1]))
    per = -(-len(order) // (side - 1))

    def extra(step):
        for turn in range(side - 1):

            @pl.when(step == turn)
            def _():
                for r, c, count in order[turn * per : (turn + 1) * per]:
                    move(r, c, count)().start()

    factor(group, lines, inverse, upper, row_ref, extra)
    lines.last()
    inv_hi[...], inv_lo[...] = split(inverse[...])

    def home(spot, mine):
        row_k = row_ps = ok = kinds = ranks = jnp.int32(0)
        for k in range(runs):
            ps = side * spot + mine - shift[k] - side * k
            valid = jnp.logical_and(ps >= 0, ps < side)
            row_k, row_ps = jnp.where(valid, k, row_k), jnp.where(valid, ps, row_ps)
            kinds, ranks = jnp.where(valid, kind[k], kinds), jnp.where(valid, rank[k], ranks)
            ok = jnp.where(valid, 1, ok)
        return row_k, row_ps, ok, kinds, ranks

    row_home = [home(t, p) for t in range(rows)]
    col_home = [home(t, q) for t in range(rows)]
    for index, (k, ps, ok, _, _) in enumerate(row_home + col_home):
        block = wide[ps, k + 1]
        tall[index // 2, (index % 2) * size : (index % 2 + 1) * size, :] = jnp.where(
            ok > 0, block, 0.0
        )

    def times(index, carry):
        value = product(split(tall[index]), (inv_hi[...], inv_lo[...]))
        at = pl.ds(pl.multiple_of(index * 2 * size, 2 * size), 2 * size)
        l_hi[at, :], l_lo[at, :] = split(value)
        return carry

    lax.fori_loop(0, rows, times, 0)
    own = pl.ds(pl.multiple_of(q * size, size), size)
    panel_ref[0] = top_block(upper, p, q, size)
    left = wide[p, 1:rows].reshape(runs * size, side * size)
    below = product(split(left), (inv_hi[own, :], inv_lo[own, :]))
    panel_ref[1:rows] = below.reshape(runs, size, size)

    for r, c, count in order:
        move(r, c, count)().wait()
    high = rows * size
    row_id = lax.broadcasted_iota(jnp.int32, (size, size), 0)
    col_id = lax.broadcasted_iota(jnp.int32, (size, size), 1)
    ranges = [(0, 1)] + [(u, min(u + 2, rows)) for u in range(1, rows, 2)]
    for first, end in ranges:
        taken = slice(first * size, high)
        given = slice(high + first * size, high + end * size)
        out = product((l_hi[taken, :], l_lo[taken, :]), (l_hi[given, :], l_lo[given, :]))
        for u in range(first, end):
            _, _, c_ok, c_kind, c_rank = col_home[u]
            for t in range(u, rows):
                _, _, r_ok, r_kind, r_rank = row_home[t]
                slot = jnp.where(r_kind == c_kind, r_rank + c_rank, 2 * r_rank + c_rank)
                block = recv[r_kind * side + c_kind, slot]
                value = jnp.where(r_ok * c_ok > 0, block, 0.0)
                value = value - out[
                    (t - first) * size : (t - first + 1) * size,
                    (u - first) * size : (u - first + 1) * size,
                ]
                if u == 0:
                    value = value + share_ref[t] * above_ref[parent, side * t + p, q].astype(f32)
                if t == u:
                    factor_here = above_ref[parent, side * t + p, side * t + q].astype(f32)
                    on = jnp.logical_and(row_id == col_id, p == q)
                    value = value + jnp.where(on, diag_ref[t] * factor_here, 0.0)
                part_ref[tri(t, u, rows)] = value
    lines.finish()
    group.finish()


def params(name, key):
    return dict(
        name=name,
        compiler_params=pltpu.CompilerParams(
            collective_id=key, has_side_effects=True, vmem_limit_bytes=60 * 2**20
        ),
    )


VM = pl.BlockSpec(memory_space=pltpu.VMEM)
SM = pl.BlockSpec(memory_space=pltpu.SMEM)
ANY = pl.BlockSpec(memory_space=pl.ANY)


def run_child(key, packed, child, parent, maps, mask, above, front, share, diag, side):
    rows, size = share.shape[0], share.shape[1]
    runs = rows - 1
    order = side * size
    lower = rows * (rows + 1) // 2
    VMEM, DMA = pltpu.VMEM, pltpu.SemaphoreType.DMA

    def body(*refs):
        leaf = lax.axis_index("leaf")
        child_kernel(packed, (leaf // child, leaf // parent), *refs)

    return pl.pallas_call(
        body,
        out_shape=(
            jax.ShapeDtypeStruct((rows, size, size), f32),
            jax.ShapeDtypeStruct((lower, size, size), f32),
        ),
        in_specs=[SM, SM, SM, ANY, VM, VM],
        out_specs=(VM, VM),
        scratch_shapes=[
            VMEM((rows, size, size), f32),
            VMEM((runs * runs, size, size), f32),
            VMEM((side * side, 4, size, size), f32),
            VMEM((side * side, 4, size, size), f32),
            VMEM((side, rows, size, order), f32),
            VMEM((order, order), f32),
            VMEM((order, order), f32),
            VMEM((size, order), f32),
            VMEM((order, order), bf16),
            VMEM((order, order), bf16),
            VMEM((rows, 2 * size, order), f32),
            VMEM((2 * rows * size, order), bf16),
            VMEM((2 * rows * size, order), bf16),
            DMA((lower,)),
            DMA((side * side,)),
            DMA((side * side,)),
            *gather_sems(side),
        ],
        **params(f"child_{key}", key),
    )(maps, mask, above, front, share, diag)


def top_kernel(
    bit,
    mine,
    early,
    panels_ref,
    top_ref,
    theirs,
    column,
    wide,
    inverse,
    upper,
    row_ref,
    inv_hi,
    inv_lo,
    l_hi,
    l_lo,
    done,
    blank,
    x_send,
    x_recv,
    out_sem,
    *sems,
):
    rows, size = column.shape[0], column.shape[1]
    runs = rows - 1
    side = wide.shape[0]
    group = Group(side, rows, size, wide, sems)
    p, q = group.p, group.q
    leaf = lax.axis_index("leaf")
    partner = leaf + bit - 2 * bit * lax.rem(leaf // bit, 2)
    places = [{"leaf": partner}, {"row": group.core}, {"row": group.far}]
    for hop in range(1, side):
        places.append({"col": lax.rem(q + hop, side)})
    meet(places)
    lower = mine.shape[0]
    cuts = [(0, 1), (1, rows), (rows, lower)]

    def trade(index):
        low, high = cuts[index]
        return lambda: group.copy(
            mine.at[low:high],
            theirs.at[low:high],
            x_send.at[index],
            x_recv.at[index],
            {"leaf": partner},
        )

    for index in range(len(cuts)):
        group.start(True, trade(index))
    blank[...] = jnp.zeros_like(blank)
    for k in range(panels_ref.shape[0] - 1):
        panels_ref[k] = early[k]
    trade(0)().wait_recv()
    column[0] = mine[0] + theirs[0]
    gather_corner(group, column)
    trade(1)().wait_recv()
    for t in range(1, rows):
        column[t] = mine[t] + theirs[t]
    wide[p, 1:rows, :, group.columns(q)] = column[1:rows]
    lines = Lines(group, column, False)
    lines.open()
    gather_strips(group)
    load_corner(group, inverse)
    factor(group, lines, inverse, upper, row_ref, lambda step: None)
    lines.last()
    inv_hi[...], inv_lo[...] = split(inverse[...])
    last = panels_ref.shape[0] - 1
    panels_ref[last, 0] = top_block(upper, p, q, size)
    own = pl.ds(pl.multiple_of(q * size, size), size)

    def times(index, carry):
        row = jnp.where(index < runs, p, q)
        t = jnp.where(index < runs, index, index - runs) + 1
        value = product(split(wide[row, t]), (inv_hi[...], inv_lo[...]))
        at = pl.ds(pl.multiple_of(index * size, size), size)
        l_hi[at, :], l_lo[at, :] = split(value)
        return carry

    lax.fori_loop(0, 2 * runs, times, 0)
    left = wide[p, 1:rows].reshape(runs * size, side * size)
    below = product(split(left), (inv_hi[own, :], inv_lo[own, :]))
    panels_ref[last, 1:rows] = below.reshape(runs, size, size)
    trade(2)().wait_recv()
    high = runs * size
    row_id = lax.broadcasted_iota(jnp.int32, (size, size), 0)
    col_id = lax.broadcasted_iota(jnp.int32, (size, size), 1)
    writes = []
    for k in range(runs):
        for l in range(runs):
            source = blank if k < l else done.at[k * runs + l]
            writes.append(
                pltpu.make_async_copy(
                    source, top_ref.at[0, k, 0, :, l, 0, :], out_sem.at[k * runs + l]
                )
            )
            if k < l:
                writes[-1].start()
    for first in range(0, runs, 2):
        end = min(first + 2, runs)
        taken = slice(first * size, high)
        given = slice(high + first * size, high + end * size)
        out = product((l_hi[taken, :], l_lo[taken, :]), (l_hi[given, :], l_lo[given, :]))
        for l in range(first, end):
            for k in range(l, runs):
                at = tri(k + 1, l + 1, rows)
                value = (mine[at] + theirs[at]) - out[
                    (k - first) * size : (k - first + 1) * size,
                    (l - first) * size : (l - first + 1) * size,
                ]
                if k == l:
                    keep = jnp.logical_or(p > q, jnp.logical_and(p == q, row_id >= col_id))
                    value = jnp.where(keep, value, 0.0)
                done[k * runs + l] = value
                writes[k * runs + l].start()
    for write in writes:
        write.wait()
    lines.finish()
    group.finish()


def run_top(key, bit, part, early, rows, side):
    size = part.shape[1]
    runs = rows - 1
    order = side * size
    VMEM, DMA = pltpu.VMEM, pltpu.SemaphoreType.DMA
    return pl.pallas_call(
        functools.partial(top_kernel, bit),
        out_shape=(
            jax.ShapeDtypeStruct((early.shape[0] + 1, rows, size, size), f32),
            jax.ShapeDtypeStruct((1, runs, 1, size, runs, 1, size), f32),
        ),
        in_specs=[VM, VM],
        out_specs=(VM, ANY),
        scratch_shapes=[
            VMEM(part.shape, f32),
            VMEM((rows, size, size), f32),
            VMEM((side, rows, size, order), f32),
            VMEM((order, order), f32),
            VMEM((order, order), f32),
            VMEM((size, order), f32),
            VMEM((order, order), bf16),
            VMEM((order, order), bf16),
            VMEM((2 * runs * size, order), bf16),
            VMEM((2 * runs * size, order), bf16),
            VMEM((runs * runs, size, size), f32),
            VMEM((size, size), f32),
            DMA((3,)),
            DMA((3,)),
            DMA((runs * runs,)),
            *gather_sems(side),
        ],
        **params(f"top_{key}", key),
    )(part, early)


def partner_2(block, axis, bit):
    count = lax.axis_size(axis)
    route = []
    for low in range(count):
        high = low | 1 << bit
        if high != low and high < count:
            route += [(low, high), (high, low)]
    return lax.ppermute(block, axis, route)


def shards(leaf_front, leaf_pattern, parent_panel, parent_diag, parent_pattern, ext_map):
    rows = leaf_front.shape[1]
    size = leaf_front.shape[3]
    levels = parent_panel.shape[0]
    side = lax.axis_size("row")
    share = parent_panel.reshape(levels, rows, size, size)
    diag = parent_diag.reshape(levels, rows, 1, size)
    front, packed = leaf_front, False
    panel_list = []
    for depth in range(levels):
        panel, part = run_child(
            depth,
            packed,
            1 << depth,
            2 << depth,
            ext_map[depth],
            leaf_pattern[0],
            parent_pattern[depth],
            front,
            share[depth],
            diag[depth],
            side,
        )
        panel_list.append(panel)
        if depth + 1 < levels:
            front = part + partner_2(part, "leaf", depth)
            packed = True
            higher = (share[depth + 1 :], diag[depth + 1 :])
            other = partner_2(higher, "leaf", depth)
            share = jnp.concatenate([share[: depth + 1], higher[0] + other[0]], axis=0)
            diag = jnp.concatenate([diag[: depth + 1], higher[1] + other[1]], axis=0)
    panels, top_update = run_top(
        levels, 1 << (levels - 1), part, jnp.stack(panel_list), rows, side
    )
    return (panels.reshape(levels + 1, 1, rows, 1, size, 1, size), top_update)


def solution(mesh):
    return jax.shard_map(
        shards,
        mesh=mesh,
        in_specs=(
            P("leaf", None, "row", None, None, "col", None),
            P("leaf", None, None),
            P(None, "leaf", None, "row", None, "col", None),
            P(None, "leaf", None, "row", None),
            P(),
            P(),
        ),
        out_specs=(
            P(None, "leaf", None, "row", None, "col", None),
            P("leaf", None, "row", None, None, "col", None),
        ),
        check_vma=False,
    )
```

```python
import functools
import jax
import jax.numpy as jnp
from jax import lax
from jax.experimental import pallas as pl
from jax.experimental.pallas import tpu as pltpu
from jax.sharding import PartitionSpec as P

highest = lax.Precision.HIGHEST
MESH = pl.DeviceIdType.MESH
f32 = jnp.float32
bf16 = jnp.bfloat16


def symmetric_lower(matrix):
    size = matrix.shape[0]
    row = lax.broadcasted_iota(jnp.int32, (size, size), 0)
    col = lax.broadcasted_iota(jnp.int32, (size, size), 1)
    return jnp.where(row >= col, matrix, matrix.T)


def eliminate_block(block):
    size = block.shape[0]
    groups = size // 8
    lane = lax.broadcasted_iota(jnp.int32, (8, size), 1)
    sub = lax.broadcasted_iota(jnp.int32, (8, size), 0)
    rows = [block[8 * g : 8 * g + 8, :] for g in range(groups)]
    for g in range(groups):
        base = 8 * g
        here = rows[g]
        inside = jnp.logical_and(lane >= base, lane < base + 8)
        line = [jnp.broadcast_to(here[a : a + 1, :], (8, size)) for a in range(8)]
        s = [
            [
                jnp.broadcast_to(line[a][:, base + b : base + b + 1], (8, size)) if b >= a else None
                for b in range(8)
            ]
            for a in range(8)
        ]
        line = [
            jnp.where(inside, jnp.where(lane == base + a, 1.0, 0.0), line[a]) for a in range(8)
        ]
        inverse = [None] * 8
        ratio = [[None] * 8 for _ in range(8)]
        for a in range(8):
            inverse[a] = 1.0 / s[a][a]
            for b in range(a + 1, 8):
                ratio[a][b] = s[a][b] * inverse[a]
            for b in range(a + 1, 8):
                for c in range(b, 8):
                    s[b][c] = s[b][c] - ratio[a][b] * s[a][c]
                line[b] = line[b] - ratio[a][b] * line[a]
        done = line[0]
        for a in range(8):
            whole = line[a]
            for b in range(a, 8):
                whole = jnp.where(lane == base + b, s[a][b], whole)
            done = whole if a == 0 else jnp.where(sub == a, whole, done)
        rows[g] = done
        if g + 1 < groups:
            solved = [None] * 8
            for a in range(7, -1, -1):
                total = line[a] * inverse[a]
                for b in range(a + 1, 8):
                    total = total - ratio[a][b] * solved[b]
                solved[a] = total
            for h in range(g + 1, groups):
                before = rows[h]
                total = jnp.where(inside, 0.0, before)
                for a in range(8):
                    spread = jnp.broadcast_to(before[:, base + a : base + a + 1], (8, size))
                    total = total - spread * solved[a]
                rows[h] = total
    return jnp.concatenate(rows, axis=0)


def pivot_step(step, size, row_of, work):
    row_ref, upper_ref, hi, lo = work
    order = hi.shape[0]
    start = pl.multiple_of(step * size, size)
    here = pl.ds(start, size)
    row_id = lax.broadcasted_iota(jnp.int32, (size, size), 0)
    col_id = lax.broadcasted_iota(jnp.int32, (size, size), 1)
    row_ref[...] = row_of(step) - three((hi[:, here], lo[:, here]), (hi[...], lo[...]), 0, 0)
    hi[:, here] = jnp.zeros((order, size), bf16)
    lo[:, here] = jnp.zeros((order, size), bf16)
    reduced = eliminate_block(row_ref[:, here])
    pivot = jnp.sum(jnp.where(row_id == col_id, reduced, 0.0), axis=1, keepdims=True)
    scale = lax.rsqrt(pivot)
    scale = scale * (1.5 - 0.5 * pivot * scale * scale)
    scaled = reduced * scale
    small = jnp.where(row_id > col_id, scaled, jnp.where(row_id == col_id, scale, 0.0))
    row_ref[...] = three(split(small), split(row_ref[...]), 1, 0)
    row_ref[:, here] = small
    row = row_ref[...]
    upper_ref[here, :] = row
    upper_ref[here, here] = jnp.where(row_id <= col_id, scaled, 0.0)
    hi[here, :], lo[here, :] = split(row)


def split(value):
    high = value.astype(bf16)
    return high, (value - high.astype(f32)).astype(bf16)


def three(left, right, left_dim, right_dim):
    dims = (((left_dim,), (right_dim,)), ((), ()))
    pairs = ((left[1], right[0]), (left[0], right[1]), (left[0], right[0]))
    parts = [lax.dot_general(a, b, dims, preferred_element_type=f32) for a, b in pairs]
    return (parts[0] + parts[1]) + parts[2]


def product(left, right):
    return three(left, right, 1, 1)


def run(when, act):
    if when is True:
        act()
    else:
        pl.when(when)(act)


class Group:
    def __init__(self, side, rows, size, wide, sems):
        self.side, self.rows, self.size, self.wide = side, rows, size, wide
        self.p = lax.axis_index("row")
        self.q = lax.axis_index("col")
        self.core = self.p + 1 - 2 * lax.rem(self.p, 2)
        self.far = lax.rem(self.p + side // 2, side)
        self.diagonal = lax.rem(self.core + side // 2, side)
        self.sems = sems
        self.sent = []

    def columns(self, source):
        return pl.ds(pl.multiple_of(source * self.size, self.size), self.size)

    def copy(self, source, target, send, receive, place):
        return pltpu.make_async_remote_copy(
            src_ref=source,
            dst_ref=target,
            send_sem=send,
            recv_sem=receive,
            device_id=place,
            device_id_type=MESH,
        )

    def start(self, when, make):
        run(when, lambda: make().start())
        self.sent.append((when, make))

    def finish(self):
        for when, make in self.sent:
            run(when, lambda: make().wait_send())
        self.sent = []

    def spot(self, row, source, part):
        if part == "corner":
            return self.wide.at[row, 0, :, self.columns(source)]
        return self.wide.at[row, 1 : self.rows, :, self.columns(source)]

    def mates(self):
        return ((0, self.core), (1, self.far), (2, self.diagonal))


class Corner:
    def __init__(self, group, column):
        self.group, self.column = group, column

    def along(self, act):
        g = self.group
        for hop in range(1, g.side):

            def make(hop=hop):
                return g.copy(
                    self.column.at[0],
                    g.spot(g.p, g.q, "corner"),
                    g.sems[0].at[hop],
                    g.sems[1].at[g.q],
                    {"col": lax.rem(g.q + hop, g.side)},
                )

            run(g.p >= g.q, lambda: act(make()))

    def piece(self, index, row, place, source):
        g = self.group
        spot = g.spot(row, source, "corner")
        return g.copy(
            spot, spot, g.sems[2].at[index, source], g.sems[3].at[index, source], {"row": place}
        )

    def open(self):
        g = self.group
        g.wide[g.p, 0, :, g.columns(g.q)] = self.column[0]
        self.along(begin)

    def spread(self):
        g = self.group
        for source in range(g.side):

            def arrive(source=source):
                spot = g.spot(g.p, source, "corner")
                g.copy(
                    spot, spot, g.sems[0].at[0], g.sems[1].at[source], {"col": g.q}
                ).wait_recv()

            run(jnp.logical_and(g.p >= source, g.q != source), arrive)
            self.across(source, begin)

    def across(self, source, act):
        g = self.group

        def body():
            for index, place in g.mates():
                act(self.piece(index, g.p, place, source))

        run(g.p >= source, body)

    def need(self, step):
        g = self.group
        for index, row in g.mates():
            run(row >= step, lambda: self.piece(index, row, g.p, step).wait_recv())

    def row(self, step):
        g = self.group
        blocks = []
        for j in range(g.side):
            block = g.wide[j, 0, :, g.columns(step)]
            blocks.append(
                jnp.where(j > step, block.T, jnp.where(j == step, symmetric_lower(block), 0.0))
            )
        return jnp.concatenate(blocks, axis=1)

    def finish(self):
        self.along(settle)
        for source in range(self.group.side):
            self.across(source, settle)


class Lines:
    def __init__(self, group, column, every):
        self.group, self.column, self.every = group, column, every

    def wanted(self, row):
        return True if self.every else row == self.group.q

    def both(self, *conditions):
        kept = [c for c in conditions if c is not True]
        return functools.reduce(jnp.logical_and, kept) if kept else True

    def inside(self, source):
        return jnp.logical_and(source >= 0, source < self.group.side)

    def hop(self, step, act):
        g = self.group
        send, receive = g.sems[4:6]
        for index, sign in ((0, 1), (1, -1)):
            source = g.q - sign * (step - 1)
            to = g.q + sign

            def make(index=index, source=source, to=to):
                spot = g.spot(g.p, source, "lines")
                return g.copy(
                    spot, spot, send.at[2 * (step - 1) + index], receive.at[source], {"col": to}
                )

            when = jnp.logical_and(self.inside(source), self.inside(to))
            run(when, lambda: act(make()))

    def arrive(self, step):
        g = self.group
        send, receive = g.sems[4:6]
        for sign in (1, -1):
            source = g.q - sign * step

            def wait(source=source):
                spot = g.spot(g.p, source, "lines")
                g.copy(spot, spot, send.at[0], receive.at[source], {"col": g.q}).wait_recv()

            run(self.inside(source), wait)

    def sources(self, step):
        out = []
        for sign in (1, -1):
            source = self.group.q - sign * step
            valid = self.inside(source)
            if sign < 0:
                valid = jnp.logical_and(valid, step > 0)
            out.append((valid, source))
        return out

    def across(self, step, act):
        g = self.group
        send, receive = g.sems[6:8]
        for valid, source in self.sources(step):
            for index, place in ((0, g.far), (1, g.core)):

                def make(index=index, place=place, source=source):
                    spot = g.spot(g.p, source, "lines")
                    return g.copy(
                        spot,
                        spot,
                        send.at[index, source],
                        receive.at[index, source],
                        {"row": place},
                    )

                run(self.both(valid, self.wanted(g.p)), lambda: act(make()))

    def pass_on(self, step, act, first):
        g = self.group
        send, receive = g.sems[6:8]
        for valid, source in self.sources(step):

            def make(source=source):
                spot = g.spot(g.far, source, "lines")
                return g.copy(
                    spot, spot, send.at[2, source], receive.at[2, source], {"row": g.core}
                )

            def whole(source=source, make=make):
                if first:
                    spot = g.spot(g.far, source, "lines")
                    g.copy(
                        spot, spot, send.at[0, source], receive.at[0, source], {"row": g.p}
                    ).wait_recv()
                act(make())

            run(self.both(valid, self.wanted(g.far)), whole)

    def last(self):
        g = self.group
        send, receive = g.sems[6:8]
        for index, row in ((1, g.core), (2, g.diagonal)):
            for source in range(g.side):

                def wait(index=index, row=row, source=source):
                    spot = g.spot(row, source, "lines")
                    g.copy(
                        spot,
                        spot,
                        send.at[index, source],
                        receive.at[index, source],
                        {"row": g.p},
                    ).wait_recv()

                run(self.wanted(row), wait)

    def open(self):
        self.hop(1, begin)
        self.across(0, begin)

    def advance(self, step):
        side = self.group.side

        @pl.when(step + 1 < side)
        def _():
            self.arrive(step + 1)

            @pl.when(step + 2 < side)
            def _():
                self.hop(step + 2, begin)

            self.across(step + 1, begin)

        self.pass_on(step, begin, True)

    def finish(self):
        def body(step, carry):
            pl.when(step > 0)(lambda: self.hop(step, settle))
            self.across(step, settle)
            self.pass_on(step, settle, False)
            return carry

        lax.fori_loop(0, self.group.side, body, 0)


def begin(copy):
    copy.start()


def settle(copy):
    copy.wait_send()


def gather_sems(side):
    return [
        pltpu.SemaphoreType.DMA((side,)),
        pltpu.SemaphoreType.DMA((side,)),
        pltpu.SemaphoreType.DMA((3, side)),
        pltpu.SemaphoreType.DMA((3, side)),
        pltpu.SemaphoreType.DMA((2 * side,)),
        pltpu.SemaphoreType.DMA((side,)),
        pltpu.SemaphoreType.DMA((3, side)),
        pltpu.SemaphoreType.DMA((3, side)),
    ]


def meet(places):
    barrier = pltpu.get_barrier_semaphore()
    for place in places:
        pl.semaphore_signal(barrier, inc=1, device_id=place, device_id_type=MESH)
    pl.semaphore_wait(barrier, len(places))


def top_block(upper_ref, p, q, size):
    block = upper_ref[
        pl.ds(pl.multiple_of(q * size, size), size), pl.ds(pl.multiple_of(p * size, size), size)
    ]
    return jnp.where(p >= q, block.T, 0.0)


def tri(row, col, rows):
    return col * rows - col * (col - 1) // 2 + row - col


def factor(group, corner, lines, work, extra):
    hi, lo = work[2:]
    hi[...] = jnp.zeros_like(hi)
    lo[...] = jnp.zeros_like(lo)

    def body(step, carry):
        corner.need(step)
        pivot_step(step, group.size, corner.row, work)
        lines.advance(step)
        extra(step)
        return carry

    lax.fori_loop(0, group.side, body, 0)


def child_phase(packed, node, front_refs, part_ref, panel_ref, refs, sems, group):
    map_ref, mask_ref, above_ref, front, share_ref, diag_ref = front_refs
    (column, inner, pack, near, late, wide, row_ref, upper, hi, lo, tall, l_hi, l_lo, table) = refs
    load_sem, n_send, n_recv, f_send, f_recv = sems
    child, parent = node
    rows, size = column.shape[0], column.shape[1]
    runs = rows - 1
    side = wide.shape[0]
    p, q = group.p, group.q

    def block_of(t, u):
        if packed:
            return front.at[tri(t, u, rows)]
        return front.at[0, t, 0, :, u, 0, :]

    def place_of(t, u):
        return column.at[t] if u == 0 else inner.at[(t - 1) * runs + u - 1]

    spots = [(t, u) for u in range(rows) for t in range(u, rows)]
    loads = [
        pltpu.make_async_copy(block_of(t, u), place_of(t, u), load_sem.at[index])
        for index, (t, u) in enumerate(spots)
    ]
    for load in loads:
        load.start()
    yield

    def masked(t, u):
        if packed:
            return 1.0
        return mask_ref[side * t + p, side * u + q].astype(f32)

    loads[0].wait()
    column[0] = column[0] * masked(0, 0)
    corner = Corner(group, column)
    corner.open()
    for t in range(1, rows):
        loads[t].wait()
        column[t] = column[t] * masked(t, 0)
    wide[p, 1:rows, :, group.columns(q)] = column[1:rows]
    lines = Lines(group, column, True)
    lines.open()
    for index in range(rows, len(spots)):
        loads[index].wait()

    shift = [jnp.clip(map_ref[child, side * k] - side * k, 0, side) for k in range(runs)]
    kind = [lax.rem(s, side) for s in shift]
    rank = []
    for k in range(runs):
        count = jnp.int32(0)
        for j in range(k):
            count = count + jnp.where(kind[j] == kind[k], 1, 0)
        rank.append(jnp.minimum(count, 1))
    for r in range(side):
        for i in range(2):
            found = jnp.int32(0)
            for k in range(runs):
                hit = jnp.logical_and(kind[k] == r, rank[k] == i)
                found = jnp.where(hit, k, found)
            table[r * 2 + i] = found

    def fill(index, carry):
        r, c = index // side, lax.rem(index, side)

        @pl.when(jnp.logical_or(r == 0, jnp.logical_or(c == 0, r >= c)))
        def _():
            for slot in range(4):
                k, l = table[r * 2 + slot % 2], table[c * 2 + slot // 2]
                k, l = jnp.maximum(k, l), jnp.minimum(k, l)
                block = inner[k * runs + l]
                if not packed:
                    mark = mask_ref[side * (k + 1) + p, side * (l + 1) + q]
                    block = block * mark.astype(f32)
                pack[index, slot] = block

        return carry

    lax.fori_loop(0, side * side, fill, 0)
    near[0] = pack[0, 0:2]
    late[0] = pack[0]

    moves = [
        (r, c)
        for c in range(side)
        for r in range(side)
        if (r or c) and (r == 0 or c == 0 or r >= c)
    ]
    ahead = [(r, c) for r, c in moves if c + 1 < side]

    def send_near(r, c):
        index = r * side + c
        return group.copy(
            pack.at[index, 0:2],
            near.at[index],
            n_send.at[index],
            n_recv.at[index],
            {"row": lax.rem(p + r, side), "col": lax.rem(q + c, side)},
        )

    def send_late(r, c):
        index = r * side + c
        first = 0 if c + 1 == side else 3 if r == c else 2
        return group.copy(
            pack.at[index, first:4],
            late.at[index, first:4],
            f_send.at[index],
            f_recv.at[index],
            {"row": lax.rem(p + r, side), "col": lax.rem(q + c, side)},
        )

    early = [(r, c) for r, c in moves if c % 2 == 0]
    other = [(r, c) for r, c in moves if c % 2]
    ahead.sort(key=lambda m: -m[1])

    def extra(step):
        @pl.when(step == max(side - 3, 0))
        def _():
            for r, c in ahead:
                send_near(r, c).start()

        @pl.when(step == side - 2)
        def _():
            for r, c in early:
                send_late(r, c).start()

    corner.spread()
    factor(group, corner, lines, (row_ref, upper, hi, lo), extra)
    lines.last()

    def home(spot, mine):
        row_k = row_ps = ok = kinds = ranks = jnp.int32(0)
        for k in range(runs):
            ps = side * spot + mine - shift[k] - side * k
            valid = jnp.logical_and(ps >= 0, ps < side)
            row_k, row_ps = jnp.where(valid, k, row_k), jnp.where(valid, ps, row_ps)
            kinds, ranks = jnp.where(valid, kind[k], kinds), jnp.where(valid, rank[k], ranks)
            ok = jnp.where(valid, 1, ok)
        return row_k, row_ps, ok, kinds, ranks

    row_home = [home(t, p) for t in range(rows)]
    col_home = [home(t, q) for t in range(rows)]
    for index, (k, ps, ok, _, _) in enumerate(row_home + col_home):
        block = wide[ps, k + 1]
        tall[index // 2, (index % 2) * size : (index % 2 + 1) * size, :] = jnp.where(
            ok > 0, block, 0.0
        )

    def times(index, carry):
        value = product(split(tall[index]), (hi[...], lo[...]))
        at = pl.ds(pl.multiple_of(index * 2 * size, 2 * size), 2 * size)
        l_hi[at, :], l_lo[at, :] = split(value)
        return carry

    count = (rows + 2) // 2
    lax.fori_loop(0, count, times, 0)
    high = rows * size
    row_id = lax.broadcasted_iota(jnp.int32, (size, size), 0)
    col_id = lax.broadcasted_iota(jnp.int32, (size, size), 1)

    def build(first, end):
        taken = slice(first * size, high)
        given = slice(high + first * size, high + end * size)
        out = product((l_hi[taken, :], l_lo[taken, :]), (l_hi[given, :], l_lo[given, :]))
        for u in range(first, end):
            _, _, c_ok, c_kind, c_rank = col_home[u]
            for t in range(u, rows):
                _, _, r_ok, r_kind, r_rank = row_home[t]
                index = r_kind * side + c_kind
                if u == 0:
                    block = near[index, r_rank]
                else:
                    ready = jnp.logical_and(c_rank == 0, c_kind + 1 < side)
                    block = jnp.where(ready, near[index, r_rank], late[index, 2 * c_rank + r_rank])
                value = jnp.where(r_ok * c_ok > 0, block, 0.0)
                value = value - out[
                    (t - first) * size : (t - first + 1) * size,
                    (u - first) * size : (u - first + 1) * size,
                ]
                if u == 0:
                    value = value + share_ref[t] * above_ref[parent, side * t + p, q].astype(f32)
                if t == u:
                    factor_here = above_ref[parent, side * t + p, side * t + q].astype(f32)
                    on = jnp.logical_and(row_id == col_id, p == q)
                    value = value + jnp.where(on, diag_ref[t] * factor_here, 0.0)
                part_ref[tri(t, u, rows)] = value

    def arrived(spot, send, receive):
        group.copy(spot, spot, send, receive, {"row": p}).wait_recv()

    for r, c in ahead:
        index = r * side + c
        arrived(near.at[index], n_send.at[0], n_recv.at[index])
    build(0, 1)
    yield

    lax.fori_loop(count, rows, times, 0)
    own = pl.ds(pl.multiple_of(q * size, size), size)
    panel_ref[0] = top_block(upper, p, q, size)
    left = wide[p, 1:rows].reshape(runs * size, side * size)
    below = product(split(left), (hi[own, :], lo[own, :]))
    panel_ref[1:rows] = below.reshape(runs, size, size)
    yield

    for r, c in other:
        send_late(r, c).start()
    yield

    for r, c in moves:
        index = r * side + c
        first = 0 if c + 1 == side else 3 if r == c else 2
        arrived(late.at[index, first:4], f_send.at[0], f_recv.at[index])
    for first in range(1, rows, 2):
        build(first, min(first + 2, rows))
        yield
    for r, c in moves:
        send_late(r, c).wait_send()
    for r, c in ahead:
        send_near(r, c).wait_send()
    corner.finish()
    lines.finish()
    yield


def params(name, key):
    return dict(
        name=name,
        compiler_params=pltpu.CompilerParams(
            collective_id=key, has_side_effects=True, vmem_limit_bytes=62 * 2**20
        ),
    )


VM = pl.BlockSpec(memory_space=pltpu.VMEM)
SM = pl.BlockSpec(memory_space=pltpu.SMEM)
ANY = pl.BlockSpec(memory_space=pl.ANY)
VMEM, DMA = pltpu.VMEM, pltpu.SemaphoreType.DMA


def child_scratch(rows, size, side):
    order = side * size
    runs = rows - 1
    return [
        VMEM((rows, size, size), f32),
        VMEM((runs * runs, size, size), f32),
        VMEM((side * side, 4, size, size), f32),
        VMEM((side * side, 2, size, size), f32),
        VMEM((side * side, 4, size, size), f32),
        VMEM((side, rows, size, order), f32),
        VMEM((size, order), f32),
        VMEM((order, order), f32),
        VMEM((order, order), bf16),
        VMEM((order, order), bf16),
        VMEM((rows, 2 * size, order), f32),
        VMEM((2 * rows * size, order), bf16),
        VMEM((2 * rows * size, order), bf16),
        pltpu.SMEM((2 * side,), jnp.int32),
    ], [
        DMA((rows * (rows + 1) // 2,)),
        DMA((side * side,)),
        DMA((side * side,)),
        DMA((side * side,)),
        DMA((side * side,)),
        *gather_sems(side),
    ]


def around(side):
    p, q = lax.axis_index("row"), lax.axis_index("col")
    return [
        {"row": lax.rem(p + r, side), "col": lax.rem(q + c, side)}
        for r in range(side)
        for c in range(side)
        if r or c
    ]


def run_child(key, packed, child, parent, inputs, side):
    rows, size = inputs[4].shape[0], inputs[4].shape[1]
    lower = rows * (rows + 1) // 2
    refs, sems = child_scratch(rows, size, side)

    def body(*args):
        panel_ref, part_ref = args[6:8]
        mine = args[8 : 8 + len(refs)]
        flags = args[8 + len(refs) :]
        leaf = lax.axis_index("leaf")
        group = Group(side, rows, size, mine[5], flags[5:])
        node = (leaf // child, leaf // parent)
        phase = child_phase(
            packed, node, args[:6], part_ref, panel_ref, mine, flags[:5], group
        )
        next(phase)
        meet(around(side))
        for _ in phase:
            pass

    return pl.pallas_call(
        body,
        out_shape=(
            jax.ShapeDtypeStruct((rows, size, size), f32),
            jax.ShapeDtypeStruct((lower, size, size), f32),
        ),
        in_specs=[SM, SM, SM, ANY, VM, VM],
        out_specs=(VM, VM),
        scratch_shapes=refs + sems,
        **params(f"child_{key}", key),
    )(*inputs)


def top_kernel(packed, child, parent, bit, side, n_refs, *args):
    front_refs, args = args[:6], args[6:]
    panels_ref, top_ref = args[:2]
    child_refs, args = args[2 : 2 + n_refs], args[2 + n_refs :]
    mine, theirs, column, wide, l_hi, l_lo, done, blank, x_send, x_recv, out_sem = args[:11]
    flags = args[11:]
    child_sems, flags = flags[:5], flags[5:]
    half = len(flags) // 2
    rows, size = column.shape[0], column.shape[1]
    runs = rows - 1
    leaf = lax.axis_index("leaf")
    partner = leaf + bit - 2 * bit * lax.rem(leaf // bit, 2)
    first_group = Group(side, rows, size, child_refs[5], flags[:half])
    phase = child_phase(
        packed,
        (leaf // child, leaf // parent),
        front_refs,
        mine,
        panels_ref.at[0],
        child_refs,
        child_sems,
        first_group,
    )
    next(phase)
    meet(around(side) + [{"leaf": partner}])
    row_ref, upper, hi, lo = child_refs[6:10]
    group = Group(side, rows, size, wide, flags[half:])
    p, q = group.p, group.q
    cuts = [(0, 1), (1, rows)]
    for u in range(1, rows, 2):
        cuts.append((cuts[-1][1], cuts[-1][1] + sum(rows - v for v in range(u, min(u + 2, rows)))))

    def trade(index):
        low, high = cuts[index]
        return group.copy(
            mine.at[low:high],
            theirs.at[low:high],
            x_send.at[index],
            x_recv.at[index],
            {"leaf": partner},
        )

    next(phase)
    trade(0).start()
    trade(1).start()
    next(phase)
    blank[...] = jnp.zeros_like(blank)
    writes = []
    for k in range(runs):
        for l in range(runs):
            source = blank if k < l else done.at[k * runs + l]
            writes.append(
                pltpu.make_async_copy(
                    source, top_ref.at[0, k, 0, :, l, 0, :], out_sem.at[k * runs + l]
                )
            )
            if k < l:
                writes[-1].start()
    trade(0).wait_recv()
    column[0] = mine[0] + theirs[0]
    corner = Corner(group, column)
    corner.open()
    corner.spread()
    trade(1).wait_recv()
    for t in range(1, rows):
        column[t] = mine[t] + theirs[t]
    wide[p, 1:rows, :, group.columns(q)] = column[1:rows]
    lines = Lines(group, column, False)
    lines.open()

    def extra(step):
        @pl.when(step == max(side - 3, 0))
        def _():
            next(phase)

    factor(group, corner, lines, (row_ref, upper, hi, lo), extra)
    for index in range(2, len(cuts)):
        next(phase)
        trade(index).start()
    lines.last()
    last = panels_ref.shape[0] - 1
    panels_ref[last, 0] = top_block(upper, p, q, size)
    own = pl.ds(pl.multiple_of(q * size, size), size)

    def times(index, carry):
        row = jnp.where(index < runs, p, q)
        t = jnp.where(index < runs, index, index - runs) + 1
        value = product(split(wide[row, t]), (hi[...], lo[...]))
        at = pl.ds(pl.multiple_of(index * size, size), size)
        l_hi[at, :], l_lo[at, :] = split(value)
        return carry

    lax.fori_loop(0, 2 * runs, times, 0)
    left = wide[p, 1:rows].reshape(runs * size, side * size)
    below = product(split(left), (hi[own, :], lo[own, :]))
    panels_ref[last, 1:rows] = below.reshape(runs, size, size)
    high = runs * size
    row_id = lax.broadcasted_iota(jnp.int32, (size, size), 0)
    col_id = lax.broadcasted_iota(jnp.int32, (size, size), 1)
    for first in range(0, runs, 2):
        end = min(first + 2, runs)
        taken = slice(first * size, high)
        given = slice(high + first * size, high + end * size)
        out = product((l_hi[taken, :], l_lo[taken, :]), (l_hi[given, :], l_lo[given, :]))
        trade(2 + first // 2).wait_recv()
        for l in range(first, end):
            for k in range(l, runs):
                at = tri(k + 1, l + 1, rows)
                value = (mine[at] + theirs[at]) - out[
                    (k - first) * size : (k - first + 1) * size,
                    (l - first) * size : (l - first + 1) * size,
                ]
                if k == l:
                    keep = jnp.logical_or(p > q, jnp.logical_and(p == q, row_id >= col_id))
                    value = jnp.where(keep, value, 0.0)
                done[k * runs + l] = value
                writes[k * runs + l].start()
    next(phase)
    for write in writes:
        write.wait()
    for index in range(len(cuts)):
        trade(index).wait_send()
    corner.finish()
    lines.finish()


def run_top(key, packed, child, parent, bit, inputs, side):
    rows, size = inputs[4].shape[0], inputs[4].shape[1]
    runs = rows - 1
    order = side * size
    lower = rows * (rows + 1) // 2
    refs, sems = child_scratch(rows, size, side)
    cuts = 2 + -(-runs // 2)
    return pl.pallas_call(
        functools.partial(top_kernel, packed, child, parent, bit, side, len(refs)),
        out_shape=(
            jax.ShapeDtypeStruct((2, rows, size, size), f32),
            jax.ShapeDtypeStruct((1, runs, 1, size, runs, 1, size), f32),
        ),
        in_specs=[SM, SM, SM, ANY, VM, VM],
        out_specs=(VM, ANY),
        scratch_shapes=[
            *refs,
            VMEM((lower, size, size), f32),
            VMEM((lower, size, size), f32),
            VMEM((rows, size, size), f32),
            VMEM((side, rows, size, order), f32),
            VMEM((2 * runs * size, order), bf16),
            VMEM((2 * runs * size, order), bf16),
            VMEM((runs * runs, size, size), f32),
            VMEM((size, size), f32),
            DMA((cuts,)),
            DMA((cuts,)),
            DMA((runs * runs,)),
            *sems,
            *gather_sems(side),
        ],
        **params(f"top_{key}", key),
    )(*inputs)


def partner_2(block, axis, bit):
    count = lax.axis_size(axis)
    route = []
    for low in range(count):
        high = low | 1 << bit
        if high != low and high < count:
            route += [(low, high), (high, low)]
    return lax.ppermute(block, axis, route)


def shards(leaf_front, leaf_pattern, parent_panel, parent_diag, parent_pattern, ext_map):
    rows = leaf_front.shape[1]
    size = leaf_front.shape[3]
    levels = parent_panel.shape[0]
    side = lax.axis_size("row")
    share = parent_panel.reshape(levels, rows, size, size)
    diag = parent_diag.reshape(levels, rows, 1, size)
    front, packed = leaf_front, False
    panel_list = []
    for depth in range(levels):
        inputs = (
            ext_map[depth],
            leaf_pattern[0],
            parent_pattern[depth],
            front,
            share[depth],
            diag[depth],
        )
        if depth + 1 == levels:
            panels, top_update = run_top(
                depth, packed, 1 << depth, 2 << depth, 1 << depth, inputs, side
            )
            break
        panel, part = run_child(depth, packed, 1 << depth, 2 << depth, inputs, side)
        panel_list.append(panel[None])
        front = part + partner_2(part, "leaf", depth)
        packed = True
        higher = (share[depth + 1 :], diag[depth + 1 :])
        other = partner_2(higher, "leaf", depth)
        share = jnp.concatenate([share[: depth + 1], higher[0] + other[0]], axis=0)
        diag = jnp.concatenate([diag[: depth + 1], higher[1] + other[1]], axis=0)
    if panel_list:
        panels = jnp.concatenate(panel_list + [panels], axis=0)
    return (panels.reshape(levels + 1, 1, rows, 1, size, 1, size), top_update)


def solution(mesh):
    return jax.shard_map(
        shards,
        mesh=mesh,
        in_specs=(
            P("leaf", None, "row", None, None, "col", None),
            P("leaf", None, None),
            P(None, "leaf", None, "row", None, "col", None),
            P(None, "leaf", None, "row", None),
            P(),
            P(),
        ),
        out_specs=(
            P(None, "leaf", None, "row", None, "col", None),
            P("leaf", None, "row", None, None, "col", None),
        ),
        check_vma=False,
    )
```

```python
import functools
import jax
import jax.numpy as jnp
from jax import lax
from jax.experimental import pallas as pl
from jax.experimental.pallas import tpu as pltpu
from jax.sharding import PartitionSpec as P

highest = lax.Precision.HIGHEST
MESH = pl.DeviceIdType.MESH
f32 = jnp.float32
bf16 = jnp.bfloat16


def symmetric_lower(matrix):
    size = matrix.shape[0]
    row = lax.broadcasted_iota(jnp.int32, (size, size), 0)
    col = lax.broadcasted_iota(jnp.int32, (size, size), 1)
    return jnp.where(row >= col, matrix, matrix.T)


def eliminate_block(block):
    size = block.shape[0]
    groups = size // 8
    lane = lax.broadcasted_iota(jnp.int32, (8, size), 1)
    sub = lax.broadcasted_iota(jnp.int32, (8, size), 0)
    rows = [block[8 * g : 8 * g + 8, :] for g in range(groups)]
    for g in range(groups):
        base = 8 * g
        here = rows[g]
        inside = jnp.logical_and(lane >= base, lane < base + 8)
        line = [jnp.broadcast_to(here[a : a + 1, :], (8, size)) for a in range(8)]
        s = [
            [
                jnp.broadcast_to(line[a][:, base + b : base + b + 1], (8, size)) if b >= a else None
                for b in range(8)
            ]
            for a in range(8)
        ]
        line = [
            jnp.where(inside, jnp.where(lane == base + a, 1.0, 0.0), line[a]) for a in range(8)
        ]
        inverse = [None] * 8
        ratio = [[None] * 8 for _ in range(8)]
        for a in range(8):
            inverse[a] = 1.0 / s[a][a]
            for b in range(a + 1, 8):
                ratio[a][b] = s[a][b] * inverse[a]
            for b in range(a + 1, 8):
                for c in range(b, 8):
                    s[b][c] = s[b][c] - ratio[a][b] * s[a][c]
                line[b] = line[b] - ratio[a][b] * line[a]
        done = line[0]
        for a in range(8):
            whole = line[a]
            for b in range(a, 8):
                whole = jnp.where(lane == base + b, s[a][b], whole)
            done = whole if a == 0 else jnp.where(sub == a, whole, done)
        rows[g] = done
        if g + 1 < groups:
            solved = [None] * 8
            for a in range(7, -1, -1):
                total = line[a] * inverse[a]
                for b in range(a + 1, 8):
                    total = total - ratio[a][b] * solved[b]
                solved[a] = total
            for h in range(g + 1, groups):
                before = rows[h]
                total = jnp.where(inside, 0.0, before)
                for a in range(8):
                    spread = jnp.broadcast_to(before[:, base + a : base + a + 1], (8, size))
                    total = total - spread * solved[a]
                rows[h] = total
    return jnp.concatenate(rows, axis=0)


def pivot_step(step, size, row_of, work):
    row_ref, upper_ref, hi, lo = work
    order = hi.shape[0]
    start = pl.multiple_of(step * size, size)
    here = pl.ds(start, size)
    row_id = lax.broadcasted_iota(jnp.int32, (size, size), 0)
    col_id = lax.broadcasted_iota(jnp.int32, (size, size), 1)
    row_ref[...] = row_of(step) - three((hi[:, here], lo[:, here]), (hi[...], lo[...]), 0, 0)
    hi[:, here] = jnp.zeros((order, size), bf16)
    lo[:, here] = jnp.zeros((order, size), bf16)
    reduced = eliminate_block(row_ref[:, here])
    pivot = jnp.sum(jnp.where(row_id == col_id, reduced, 0.0), axis=1, keepdims=True)
    scale = lax.rsqrt(pivot)
    scale = scale * (1.5 - 0.5 * pivot * scale * scale)
    scaled = reduced * scale
    small = jnp.where(row_id > col_id, scaled, jnp.where(row_id == col_id, scale, 0.0))
    row_ref[...] = three(split(small), split(row_ref[...]), 1, 0)
    row_ref[:, here] = small
    row = row_ref[...]
    upper_ref[here, :] = row
    upper_ref[here, here] = jnp.where(row_id <= col_id, scaled, 0.0)
    hi[here, :], lo[here, :] = split(row)


def split(value):
    high = value.astype(bf16)
    return high, (value - high.astype(f32)).astype(bf16)


def three(left, right, left_dim, right_dim):
    dims = (((left_dim,), (right_dim,)), ((), ()))
    pairs = ((left[1], right[0]), (left[0], right[1]), (left[0], right[0]))
    parts = [lax.dot_general(a, b, dims, preferred_element_type=f32) for a, b in pairs]
    return (parts[0] + parts[1]) + parts[2]


def product(left, right):
    return three(left, right, 1, 1)


def run(when, act):
    if when is True:
        act()
    else:
        pl.when(when)(act)


class Group:
    def __init__(self, side, rows, size, wide, sems):
        self.side, self.rows, self.size, self.wide = side, rows, size, wide
        self.p = lax.axis_index("row")
        self.q = lax.axis_index("col")
        self.core = self.p + 1 - 2 * lax.rem(self.p, 2)
        self.far = lax.rem(self.p + side // 2, side)
        self.diagonal = lax.rem(self.core + side // 2, side)
        self.sems = sems
        self.sent = []

    def columns(self, source):
        return pl.ds(pl.multiple_of(source * self.size, self.size), self.size)

    def copy(self, source, target, send, receive, place):
        return pltpu.make_async_remote_copy(
            src_ref=source,
            dst_ref=target,
            send_sem=send,
            recv_sem=receive,
            device_id=place,
            device_id_type=MESH,
        )

    def start(self, when, make):
        run(when, lambda: make().start())
        self.sent.append((when, make))

    def finish(self):
        for when, make in self.sent:
            run(when, lambda: make().wait_send())
        self.sent = []

    def spot(self, row, source, part):
        if part == "corner":
            return self.wide.at[row, 0, :, self.columns(source)]
        return self.wide.at[row, 1 : self.rows, :, self.columns(source)]

    def mates(self):
        return ((0, self.core), (1, self.far), (2, self.diagonal))


class Corner:
    def __init__(self, group, column):
        self.group, self.column = group, column

    def along(self, act):
        g = self.group
        for hop in range(1, g.side):

            def make(hop=hop):
                return g.copy(
                    self.column.at[0],
                    g.spot(g.p, g.q, "corner"),
                    g.sems[0].at[hop],
                    g.sems[1].at[g.q],
                    {"col": lax.rem(g.q + hop, g.side)},
                )

            run(g.p >= g.q, lambda: act(make()))

    def piece(self, index, row, place, source):
        g = self.group
        spot = g.spot(row, source, "corner")
        return g.copy(
            spot, spot, g.sems[2].at[index, source], g.sems[3].at[index, source], {"row": place}
        )

    def open(self):
        g = self.group
        g.wide[g.p, 0, :, g.columns(g.q)] = self.column[0]
        self.along(begin)

    def spread(self):
        g = self.group
        for source in range(g.side):

            def arrive(source=source):
                spot = g.spot(g.p, source, "corner")
                g.copy(
                    spot, spot, g.sems[0].at[0], g.sems[1].at[source], {"col": g.q}
                ).wait_recv()

            run(jnp.logical_and(g.p >= source, g.q != source), arrive)
            self.across(source, begin)

    def across(self, source, act):
        g = self.group

        def body():
            for index, place in g.mates():
                act(self.piece(index, g.p, place, source))

        run(g.p >= source, body)

    def need(self, step):
        g = self.group
        for index, row in g.mates():
            run(row >= step, lambda: self.piece(index, row, g.p, step).wait_recv())

    def row(self, step):
        g = self.group
        blocks = []
        for j in range(g.side):
            block = g.wide[j, 0, :, g.columns(step)]
            blocks.append(
                jnp.where(j > step, block.T, jnp.where(j == step, symmetric_lower(block), 0.0))
            )
        return jnp.concatenate(blocks, axis=1)

    def finish(self):
        self.along(settle)
        for source in range(self.group.side):
            self.across(source, settle)


class Lines:
    def __init__(self, group, column, every):
        self.group, self.column, self.every = group, column, every

    def wanted(self, row):
        return True if self.every else row == self.group.q

    def both(self, *conditions):
        kept = [c for c in conditions if c is not True]
        return functools.reduce(jnp.logical_and, kept) if kept else True

    def inside(self, source):
        return jnp.logical_and(source >= 0, source < self.group.side)

    def hop(self, step, act):
        g = self.group
        send, receive = g.sems[4:6]
        for index, sign in ((0, 1), (1, -1)):
            source = g.q - sign * (step - 1)
            to = g.q + sign

            def make(index=index, source=source, to=to):
                spot = g.spot(g.p, source, "lines")
                return g.copy(
                    spot, spot, send.at[2 * (step - 1) + index], receive.at[source], {"col": to}
                )

            when = jnp.logical_and(self.inside(source), self.inside(to))
            run(when, lambda: act(make()))

    def arrive(self, step):
        g = self.group
        send, receive = g.sems[4:6]
        for sign in (1, -1):
            source = g.q - sign * step

            def wait(source=source):
                spot = g.spot(g.p, source, "lines")
                g.copy(spot, spot, send.at[0], receive.at[source], {"col": g.q}).wait_recv()

            run(self.inside(source), wait)

    def sources(self, step):
        out = []
        for sign in (1, -1):
            source = self.group.q - sign * step
            valid = self.inside(source)
            if sign < 0:
                valid = jnp.logical_and(valid, step > 0)
            out.append((valid, source))
        return out

    def across(self, step, act):
        g = self.group
        send, receive = g.sems[6:8]
        for valid, source in self.sources(step):
            for index, place in ((0, g.far), (1, g.core)):

                def make(index=index, place=place, source=source):
                    spot = g.spot(g.p, source, "lines")
                    return g.copy(
                        spot,
                        spot,
                        send.at[index, source],
                        receive.at[index, source],
                        {"row": place},
                    )

                run(self.both(valid, self.wanted(g.p)), lambda: act(make()))

    def pass_on(self, step, act, first):
        g = self.group
        send, receive = g.sems[6:8]
        for valid, source in self.sources(step):

            def make(source=source):
                spot = g.spot(g.far, source, "lines")
                return g.copy(
                    spot, spot, send.at[2, source], receive.at[2, source], {"row": g.core}
                )

            def whole(source=source, make=make):
                if first:
                    spot = g.spot(g.far, source, "lines")
                    g.copy(
                        spot, spot, send.at[0, source], receive.at[0, source], {"row": g.p}
                    ).wait_recv()
                act(make())

            run(self.both(valid, self.wanted(g.far)), whole)

    def last(self):
        g = self.group
        send, receive = g.sems[6:8]
        self.pass_on(g.side - 1, begin, True)
        for index, row in ((1, g.core), (2, g.diagonal)):
            for source in range(g.side):

                def wait(index=index, row=row, source=source):
                    spot = g.spot(row, source, "lines")
                    g.copy(
                        spot,
                        spot,
                        send.at[index, source],
                        receive.at[index, source],
                        {"row": g.p},
                    ).wait_recv()

                run(self.wanted(row), wait)

    def open(self):
        self.across(0, begin)

    def advance(self, step):
        side = self.group.side

        @pl.when(step + 1 < side)
        def _():
            self.arrive(step + 1)

            @pl.when(step + 2 < side)
            def _():
                self.hop(step + 2, begin)

            self.across(step + 1, begin)

    def lag(self, step):
        pl.when(step > 0)(lambda: self.pass_on(step - 1, begin, True))

    def finish(self):
        def body(step, carry):
            pl.when(step > 0)(lambda: self.hop(step, settle))
            self.across(step, settle)
            self.pass_on(step, settle, False)
            return carry

        lax.fori_loop(0, self.group.side, body, 0)


def begin(copy):
    copy.start()


def settle(copy):
    copy.wait_send()


def gather_sems(side):
    return [
        pltpu.SemaphoreType.DMA((side,)),
        pltpu.SemaphoreType.DMA((side,)),
        pltpu.SemaphoreType.DMA((3, side)),
        pltpu.SemaphoreType.DMA((3, side)),
        pltpu.SemaphoreType.DMA((2 * side,)),
        pltpu.SemaphoreType.DMA((side,)),
        pltpu.SemaphoreType.DMA((3, side)),
        pltpu.SemaphoreType.DMA((3, side)),
    ]


def meet(places):
    barrier = pltpu.get_barrier_semaphore()
    for place in places:
        pl.semaphore_signal(barrier, inc=1, device_id=place, device_id_type=MESH)
    pl.semaphore_wait(barrier, len(places))


def top_block(upper_ref, p, q, size):
    block = upper_ref[
        pl.ds(pl.multiple_of(q * size, size), size), pl.ds(pl.multiple_of(p * size, size), size)
    ]
    return jnp.where(p >= q, block.T, 0.0)


def tri(row, col, rows):
    return col * rows - col * (col - 1) // 2 + row - col


def factor(group, corner, lines, work, extra):
    hi, lo = work[2:]
    hi[...] = jnp.zeros_like(hi)
    lo[...] = jnp.zeros_like(lo)

    def body(step, carry):
        corner.need(step)
        pivot_step(step, group.size, corner.row, work)
        lines.advance(step)
        extra(step)
        lines.lag(step)
        return carry

    lax.fori_loop(0, group.side, body, 0)


def child_phase(packed, node, front_refs, part_ref, panel_ref, refs, sems, group):
    map_ref, mask_ref, above_ref, front, share_ref, diag_ref = front_refs
    (column, inner, pack, near, late, wide, row_ref, upper, hi, lo, tall, l_hi, l_lo, table) = refs
    load_sem, n_send, n_recv, f_send, f_recv = sems
    child, parent = node
    rows, size = column.shape[0], column.shape[1]
    runs = rows - 1
    side = wide.shape[0]
    p, q = group.p, group.q

    def block_of(t, u):
        if packed:
            return front.at[tri(t, u, rows)]
        return front.at[0, t, 0, :, u, 0, :]

    def place_of(t, u):
        return column.at[t] if u == 0 else inner.at[(t - 1) * runs + u - 1]

    spots = [(t, u) for u in range(rows) for t in range(u, rows)]
    loads = [
        pltpu.make_async_copy(block_of(t, u), place_of(t, u), load_sem.at[index])
        for index, (t, u) in enumerate(spots)
    ]
    for load in loads:
        load.start()
    yield

    def masked(t, u):
        if packed:
            return 1.0
        return mask_ref[side * t + p, 0, side * u + q].astype(f32)

    loads[0].wait()
    column[0] = column[0] * masked(0, 0)
    corner = Corner(group, column)
    corner.open()
    for t in range(1, rows):
        loads[t].wait()
        column[t] = column[t] * masked(t, 0)
    wide[p, 1:rows, :, group.columns(q)] = column[1:rows]
    lines = Lines(group, column, True)
    lines.hop(1, begin)
    for index in range(rows, len(spots)):
        loads[index].wait()

    shift = [jnp.clip(map_ref[child, side * k] - side * k, 0, side) for k in range(runs)]
    kind = [lax.rem(s, side) for s in shift]
    rank = []
    for k in range(runs):
        count = jnp.int32(0)
        for j in range(k):
            count = count + jnp.where(kind[j] == kind[k], 1, 0)
        rank.append(jnp.minimum(count, 1))
    for r in range(side):
        for i in range(2):
            found = jnp.int32(0)
            for k in range(runs):
                hit = jnp.logical_and(kind[k] == r, rank[k] == i)
                found = jnp.where(hit, k, found)
            table[r * 2 + i] = found

    def fill(index, carry):
        r, c = index // side, lax.rem(index, side)

        @pl.when(jnp.logical_or(r == 0, jnp.logical_or(c == 0, r >= c)))
        def _():
            for slot in range(4):
                k, l = table[r * 2 + slot % 2], table[c * 2 + slot // 2]
                k, l = jnp.maximum(k, l), jnp.minimum(k, l)
                block = inner[k * runs + l]
                if not packed:
                    mark = mask_ref[side * (k + 1) + p, 0, side * (l + 1) + q]
                    block = block * mark.astype(f32)
                pack[index, slot] = block

        return carry

    lax.fori_loop(0, side * side, fill, 0)
    near[0] = pack[0, 0:2]
    late[0] = pack[0]

    moves = [
        (r, c)
        for c in range(side)
        for r in range(side)
        if (r or c) and (r == 0 or c == 0 or r >= c)
    ]
    ahead = [(r, c) for r, c in moves if c + 1 < side]

    def send_near(r, c):
        index = r * side + c
        return group.copy(
            pack.at[index, 0:2],
            near.at[index],
            n_send.at[index],
            n_recv.at[index],
            {"row": lax.rem(p + r, side), "col": lax.rem(q + c, side)},
        )

    def send_late(r, c):
        index = r * side + c
        first = 0 if c + 1 == side else 3 if r == c else 2
        return group.copy(
            pack.at[index, first:4],
            late.at[index, first:4],
            f_send.at[index],
            f_recv.at[index],
            {"row": lax.rem(p + r, side), "col": lax.rem(q + c, side)},
        )

    early = [(r, c) for r, c in moves if c % 2 == 0]
    other = [(r, c) for r, c in moves if c % 2]
    ahead.sort(key=lambda m: -m[1])

    def extra(step):
        @pl.when(step == max(side - 3, 0))
        def _():
            for r, c in ahead:
                send_near(r, c).start()

        @pl.when(step == side - 2)
        def _():
            for r, c in early:
                send_late(r, c).start()

    corner.spread()
    lines.open()
    factor(group, corner, lines, (row_ref, upper, hi, lo), extra)
    lines.last()

    def home(spot, mine):
        row_k = row_ps = ok = kinds = ranks = jnp.int32(0)
        for k in range(runs):
            ps = side * spot + mine - shift[k] - side * k
            valid = jnp.logical_and(ps >= 0, ps < side)
            row_k, row_ps = jnp.where(valid, k, row_k), jnp.where(valid, ps, row_ps)
            kinds, ranks = jnp.where(valid, kind[k], kinds), jnp.where(valid, rank[k], ranks)
            ok = jnp.where(valid, 1, ok)
        return row_k, row_ps, ok, kinds, ranks

    row_home = [home(t, p) for t in range(rows)]
    col_home = [home(t, q) for t in range(rows)]
    for index, (k, ps, ok, _, _) in enumerate(row_home + col_home):
        block = wide[ps, k + 1]
        tall[index // 2, (index % 2) * size : (index % 2 + 1) * size, :] = jnp.where(
            ok > 0, block, 0.0
        )

    def times(index, carry):
        value = product(split(tall[index]), (hi[...], lo[...]))
        at = pl.ds(pl.multiple_of(index * 2 * size, 2 * size), 2 * size)
        l_hi[at, :], l_lo[at, :] = split(value)
        return carry

    count = (rows + 2) // 2
    lax.fori_loop(0, count, times, 0)
    high = rows * size
    row_id = lax.broadcasted_iota(jnp.int32, (size, size), 0)
    col_id = lax.broadcasted_iota(jnp.int32, (size, size), 1)

    def build(first, end):
        taken = slice(first * size, high)
        given = slice(high + first * size, high + end * size)
        out = product((l_hi[taken, :], l_lo[taken, :]), (l_hi[given, :], l_lo[given, :]))
        for u in range(first, end):
            _, _, c_ok, c_kind, c_rank = col_home[u]
            for t in range(u, rows):
                _, _, r_ok, r_kind, r_rank = row_home[t]
                index = r_kind * side + c_kind
                if u == 0:
                    block = near[index, r_rank]
                else:
                    ready = jnp.logical_and(c_rank == 0, c_kind + 1 < side)
                    block = jnp.where(ready, near[index, r_rank], late[index, 2 * c_rank + r_rank])
                value = jnp.where(r_ok * c_ok > 0, block, 0.0)
                value = value - out[
                    (t - first) * size : (t - first + 1) * size,
                    (u - first) * size : (u - first + 1) * size,
                ]
                if u == 0:
                    value = value + share_ref[t] * above_ref[side * t + p, parent, q].astype(f32)
                if t == u:
                    factor_here = above_ref[side * t + p, parent, side * t + q].astype(f32)
                    on = jnp.logical_and(row_id == col_id, p == q)
                    value = value + jnp.where(on, diag_ref[t] * factor_here, 0.0)
                part_ref[tri(t, u, rows)] = value

    def arrived(spot, send, receive):
        group.copy(spot, spot, send, receive, {"row": p}).wait_recv()

    for r, c in ahead:
        index = r * side + c
        arrived(near.at[index], n_send.at[0], n_recv.at[index])
    build(0, 1)
    yield

    lax.fori_loop(count, rows, times, 0)
    own = pl.ds(pl.multiple_of(q * size, size), size)
    panel_ref[0] = top_block(upper, p, q, size)
    left = wide[p, 1:rows].reshape(runs * size, side * size)
    below = product(split(left), (hi[own, :], lo[own, :]))
    panel_ref[1:rows] = below.reshape(runs, size, size)
    yield

    for r, c in other:
        send_late(r, c).start()
    yield

    for r, c in moves:
        index = r * side + c
        first = 0 if c + 1 == side else 3 if r == c else 2
        arrived(late.at[index, first:4], f_send.at[0], f_recv.at[index])
    for first in range(1, rows, 2):
        build(first, min(first + 2, rows))
        yield
    for r, c in moves:
        send_late(r, c).wait_send()
    for r, c in ahead:
        send_near(r, c).wait_send()
    corner.finish()
    lines.finish()
    yield


def params(name, key):
    return dict(
        name=name,
        compiler_params=pltpu.CompilerParams(
            collective_id=key, has_side_effects=True, vmem_limit_bytes=62 * 2**20
        ),
    )


VM = pl.BlockSpec(memory_space=pltpu.VMEM)
SM = pl.BlockSpec(memory_space=pltpu.SMEM)
ANY = pl.BlockSpec(memory_space=pl.ANY)
VMEM, DMA = pltpu.VMEM, pltpu.SemaphoreType.DMA


def child_scratch(rows, size, side):
    order = side * size
    runs = rows - 1
    return [
        VMEM((rows, size, size), f32),
        VMEM((runs * runs, size, size), f32),
        VMEM((side * side, 4, size, size), f32),
        VMEM((side * side, 2, size, size), f32),
        VMEM((side * side, 4, size, size), f32),
        VMEM((side, rows, size, order), f32),
        VMEM((size, order), f32),
        VMEM((order, order), f32),
        VMEM((order, order), bf16),
        VMEM((order, order), bf16),
        VMEM((rows, 2 * size, order), f32),
        VMEM((2 * rows * size, order), bf16),
        VMEM((2 * rows * size, order), bf16),
        pltpu.SMEM((2 * side,), jnp.int32),
    ], [
        DMA((rows * (rows + 1) // 2,)),
        DMA((side * side,)),
        DMA((side * side,)),
        DMA((side * side,)),
        DMA((side * side,)),
        *gather_sems(side),
    ]


def around(side):
    p, q = lax.axis_index("row"), lax.axis_index("col")
    return [
        {"row": lax.rem(p + r, side), "col": lax.rem(q + c, side)}
        for r in range(side)
        for c in range(side)
        if r or c
    ]


def run_child(key, packed, child, parent, inputs, side):
    rows, size = inputs[4].shape[0], inputs[4].shape[1]
    lower = rows * (rows + 1) // 2
    refs, sems = child_scratch(rows, size, side)

    def body(*args):
        panel_ref, part_ref = args[6:8]
        mine = args[8 : 8 + len(refs)]
        flags = args[8 + len(refs) :]
        leaf = lax.axis_index("leaf")
        group = Group(side, rows, size, mine[5], flags[5:])
        node = (leaf // child, leaf // parent)
        phase = child_phase(
            packed, node, args[:6], part_ref, panel_ref, mine, flags[:5], group
        )
        next(phase)
        meet(around(side))
        for _ in phase:
            pass

    return pl.pallas_call(
        body,
        out_shape=(
            jax.ShapeDtypeStruct((rows, size, size), f32),
            jax.ShapeDtypeStruct((lower, size, size), f32),
        ),
        in_specs=[SM, SM, SM, ANY, VM, VM],
        out_specs=(VM, VM),
        scratch_shapes=refs + sems,
        **params(f"child_{key}", key),
    )(*inputs)


def top_kernel(packed, child, parent, bit, side, n_refs, *args):
    front_refs, args = args[:6], args[6:]
    panels_ref, top_ref = args[:2]
    child_refs, args = args[2 : 2 + n_refs], args[2 + n_refs :]
    mine, theirs, column, wide, l_hi, l_lo, done, blank, x_send, x_recv, out_sem = args[:11]
    flags = args[11:]
    child_sems, flags = flags[:5], flags[5:]
    half = len(flags) // 2
    rows, size = column.shape[0], column.shape[1]
    runs = rows - 1
    leaf = lax.axis_index("leaf")
    partner = leaf + bit - 2 * bit * lax.rem(leaf // bit, 2)
    first_group = Group(side, rows, size, child_refs[5], flags[:half])
    phase = child_phase(
        packed,
        (leaf // child, leaf // parent),
        front_refs,
        mine,
        panels_ref.at[0],
        child_refs,
        child_sems,
        first_group,
    )
    next(phase)
    meet(around(side) + [{"leaf": partner}])
    row_ref, upper, hi, lo = child_refs[6:10]
    group = Group(side, rows, size, wide, flags[half:])
    p, q = group.p, group.q
    cuts = [(0, 1), (1, rows)]
    for u in range(1, rows, 2):
        cuts.append((cuts[-1][1], cuts[-1][1] + sum(rows - v for v in range(u, min(u + 2, rows)))))

    def trade(index):
        low, high = cuts[index]
        return group.copy(
            mine.at[low:high],
            theirs.at[low:high],
            x_send.at[index],
            x_recv.at[index],
            {"leaf": partner},
        )

    next(phase)
    trade(0).start()
    trade(1).start()
    next(phase)
    blank[...] = jnp.zeros_like(blank)
    writes = []
    for k in range(runs):
        for l in range(runs):
            source = blank if k < l else done.at[k * runs + l]
            writes.append(
                pltpu.make_async_copy(
                    source, top_ref.at[0, k, 0, :, l, 0, :], out_sem.at[k * runs + l]
                )
            )
            if k < l:
                writes[-1].start()
    trade(0).wait_recv()
    column[0] = mine[0] + theirs[0]
    corner = Corner(group, column)
    corner.open()
    corner.spread()
    trade(1).wait_recv()
    for t in range(1, rows):
        column[t] = mine[t] + theirs[t]
    wide[p, 1:rows, :, group.columns(q)] = column[1:rows]
    lines = Lines(group, column, False)
    lines.hop(1, begin)
    lines.open()

    def extra(step):
        @pl.when(step == max(side - 3, 0))
        def _():
            next(phase)

    factor(group, corner, lines, (row_ref, upper, hi, lo), extra)
    for index in range(2, len(cuts)):
        next(phase)
        trade(index).start()
    lines.last()
    last = panels_ref.shape[0] - 1
    panels_ref[last, 0] = top_block(upper, p, q, size)
    own = pl.ds(pl.multiple_of(q * size, size), size)

    pair = 2 - runs % 2
    turns = runs // pair

    def times(index, carry):
        row = jnp.where(index < turns, p, q)
        t = jnp.where(index < turns, index, index - turns) * pair + 1
        blocks = wide[row, pl.ds(t, pair)].reshape(pair * size, side * size)
        value = product(split(blocks), (hi[...], lo[...]))
        at = pl.ds(pl.multiple_of(index * pair * size, pair * size), pair * size)
        l_hi[at, :], l_lo[at, :] = split(value)
        return carry

    lax.fori_loop(0, 2 * turns, times, 0)
    left = wide[p, 1:rows].reshape(runs * size, side * size)
    below = product(split(left), (hi[own, :], lo[own, :]))
    panels_ref[last, 1:rows] = below.reshape(runs, size, size)
    high = runs * size
    row_id = lax.broadcasted_iota(jnp.int32, (size, size), 0)
    col_id = lax.broadcasted_iota(jnp.int32, (size, size), 1)
    for first in range(0, runs, 2):
        end = min(first + 2, runs)
        taken = slice(first * size, high)
        given = slice(high + first * size, high + end * size)
        out = product((l_hi[taken, :], l_lo[taken, :]), (l_hi[given, :], l_lo[given, :]))
        trade(2 + first // 2).wait_recv()
        for l in range(first, end):
            for k in range(l, runs):
                at = tri(k + 1, l + 1, rows)
                value = (mine[at] + theirs[at]) - out[
                    (k - first) * size : (k - first + 1) * size,
                    (l - first) * size : (l - first + 1) * size,
                ]
                if k == l:
                    keep = jnp.logical_or(p > q, jnp.logical_and(p == q, row_id >= col_id))
                    value = jnp.where(keep, value, 0.0)
                done[k * runs + l] = value
                writes[k * runs + l].start()
    next(phase)
    for write in writes:
        write.wait()
    for index in range(len(cuts)):
        trade(index).wait_send()
    corner.finish()
    lines.finish()


def run_top(key, packed, child, parent, bit, inputs, side):
    rows, size = inputs[4].shape[0], inputs[4].shape[1]
    runs = rows - 1
    order = side * size
    lower = rows * (rows + 1) // 2
    refs, sems = child_scratch(rows, size, side)
    cuts = 2 + -(-runs // 2)
    return pl.pallas_call(
        functools.partial(top_kernel, packed, child, parent, bit, side, len(refs)),
        out_shape=(
            jax.ShapeDtypeStruct((2, rows, size, size), f32),
            jax.ShapeDtypeStruct((1, runs, 1, size, runs, 1, size), f32),
        ),
        in_specs=[SM, SM, SM, ANY, VM, VM],
        out_specs=(VM, ANY),
        scratch_shapes=[
            *refs,
            VMEM((lower, size, size), f32),
            VMEM((lower, size, size), f32),
            VMEM((rows, size, size), f32),
            VMEM((side, rows, size, order), f32),
            VMEM((2 * runs * size, order), bf16),
            VMEM((2 * runs * size, order), bf16),
            VMEM((runs * runs, size, size), f32),
            VMEM((size, size), f32),
            DMA((cuts,)),
            DMA((cuts,)),
            DMA((runs * runs,)),
            *sems,
            *gather_sems(side),
        ],
        **params(f"top_{key}", key),
    )(*inputs)


def partner_2(block, axis, bit):
    count = lax.axis_size(axis)
    route = []
    for low in range(count):
        high = low | 1 << bit
        if high != low and high < count:
            route += [(low, high), (high, low)]
    return lax.ppermute(block, axis, route)


def shards(leaf_front, leaf_pattern, parent_panel, parent_diag, parent_pattern, ext_map):
    rows = leaf_front.shape[1]
    size = leaf_front.shape[3]
    levels = parent_panel.shape[0]
    side = lax.axis_size("row")
    share = parent_panel.reshape(levels, rows, size, size)
    diag = parent_diag.reshape(levels, rows, 1, size)
    front, packed = leaf_front, False
    panel_list = []
    for depth in range(levels):
        inputs = (
            ext_map[depth],
            leaf_pattern.transpose(1, 0, 2),
            parent_pattern[depth].transpose(1, 0, 2),
            front,
            share[depth],
            diag[depth],
        )
        if depth + 1 == levels:
            panels, top_update = run_top(
                depth, packed, 1 << depth, 2 << depth, 1 << depth, inputs, side
            )
            break
        panel, part = run_child(depth, packed, 1 << depth, 2 << depth, inputs, side)
        panel_list.append(panel[None])
        front = part + partner_2(part, "leaf", depth)
        packed = True
        higher = (share[depth + 1 :], diag[depth + 1 :])
        other = partner_2(higher, "leaf", depth)
        share = jnp.concatenate([share[: depth + 1], higher[0] + other[0]], axis=0)
        diag = jnp.concatenate([diag[: depth + 1], higher[1] + other[1]], axis=0)
    if panel_list:
        panels = jnp.concatenate(panel_list + [panels], axis=0)
    return (panels.reshape(levels + 1, 1, rows, 1, size, 1, size), top_update)


def solution(mesh):
    return jax.shard_map(
        shards,
        mesh=mesh,
        in_specs=(
            P("leaf", None, "row", None, None, "col", None),
            P("leaf", None, None),
            P(None, "leaf", None, "row", None, "col", None),
            P(None, "leaf", None, "row", None),
            P(),
            P(),
        ),
        out_specs=(
            P(None, "leaf", None, "row", None, "col", None),
            P("leaf", None, "row", None, None, "col", None),
        ),
        check_vma=False,
    )
```
